1024 devices in a mesh: dp: 4 (over x), ctx: 4 (over y_lo, core), exp: 64 (over z, y_hi).
Axes of the slice: x: 4, y: 4 (y_hi: 2, y_lo: 2; y = y_hi * 2 + y_lo), z: 32, core: 2. Of those that a mesh axis runs over, the one named last changes fastest.
Arguments:
- queries: bfloat16 [4, 1024, 3584], P('dp', 'ctx'), may hold values from -20 to 20
- keys: bfloat16 [4, 1024, 512], P('dp', 'ctx'), may hold values from -20 to 20
- values: bfloat16 [4, 1024, 512], P('dp', 'ctx'), may hold values from -6 to 6
- residual: bfloat16 [4, 1024, 3584], P('dp', 'ctx'), may hold values from -4 to 4
- labels: int32 [4, 8], P('dp'), may hold values from 0 to 1, as said below
- block_mask: int32 [4, 8, 8], P('dp'), may hold values from 0 to 1, as said below
- gains: float32 [2, 3584], replicated, may hold values from 0.5 to 1.5
- w_gate: bfloat16 [3584, 19456], P(None, 'exp'), may hold values from -0.09375 to 0.09375
- w_up: bfloat16 [3584, 19456], P(None, 'exp'), may hold values from -0.09375 to 0.09375
- w_down: bfloat16 [19456, 3584], P('exp'), may hold values from -0.15625 to 0.15625
Outputs:
- layer_out: bfloat16 [4, 1024, 3584], P('dp', ('ctx', 'exp'))
The draws below stay inside these ranges and needn't reach their ends.
Inputs may be any that keep to these rules, and one draw needn't show every extreme that they name: `labels`: per sequence a share of visual blocks is drawn, then each block's label independently. Each sequence is packed with documents made of whole blocks, the first starting at block 0. block_mask[i, j] is 1 exactly when blocks i and j lie in the same document and (j <= i, or blocks i and j are both visual with no text block between them); the diagonal is always 1.
All inputs are finite; a program needn't handle non-finite values.
Results may differ from the reference program's by a relative error of at most 0.0069.
Values may be sent and summed in bfloat16 or wider, within the bound.
A program may use at most 64 MiB of HBM per device.

```python
import jax
import jax.numpy as jnp
from jax import lax

D = 3584
HEADS = 28
KV_HEADS = 4
HEAD_DIM = 128
BLOCK = 128
LEN = 1024
NBLK = 8
FFW = 9728
N_DP = 4


def block_layout(key):
    first, second = jax.random.split(jax.random.fold_in(key, 11))
    third = jax.random.fold_in(key, 23)
    share = jax.random.randint(first, (N_DP, 1), 20, 81)
    rolls = jax.random.randint(second, (N_DP, NBLK), 0, 100)
    labels = (rolls < share).astype(jnp.int32)
    order = jnp.arange(NBLK, dtype=jnp.int32)
    starts = (jax.random.randint(third, (N_DP, NBLK), 0, 4) == 0).astype(jnp.int32)
    starts = jnp.where(order[None, :] == 0, 0, starts)
    documents = jnp.cumsum(starts, axis=1)
    same_doc = documents[:, :, None] == documents[:, None, :]
    runs = jnp.cumsum(1 - labels, axis=1)
    causal = order[None, :, None] >= order[None, None, :]
    joined = (labels[:, :, None] == 1) & (labels[:, None, :] == 1) & (runs[:, :, None] == runs[:, None, :])
    return (labels, ((causal | joined) & same_doc).astype(jnp.int32))


def draw_labels(key, part):
    return block_layout(key)[0]


def draw_block_mask(key, part):
    return block_layout(key)[1]


def query_key_pair(key):
    kq, kk = jax.random.split(jax.random.fold_in(key, 7), 2)
    kv_width = KV_HEADS * HEAD_DIM
    queries = jnp.clip(jax.random.normal(kq, (N_DP, LEN, D), jnp.float32), -6.0, 6.0)
    keys = jnp.clip(jax.random.normal(kk, (N_DP, LEN, kv_width), jnp.float32), -6.0, 6.0)
    return (queries, keys)


def draw_queries(key, part):
    return query_key_pair(key)[0].astype(jnp.bfloat16)


def draw_keys(key, part):
    return query_key_pair(key)[1].astype(jnp.bfloat16)


def steps_of(key, shape, cuts, smallest, top_value):
    gain, own = 1.0, jax.random.fold_in(key, 6)
    for dim, shards_of in cuts:
        draws = jnp.exp(jax.random.uniform(jax.random.fold_in(own, dim), (shards_of,), jnp.float32, smallest / len(cuts), top_value / len(cuts)))
        gain = gain * jnp.repeat(draws, shape[dim] // shards_of).reshape([-1 if axis == dim else 1 for axis in range(len(shape))])
    return gain


def centred(stream_key, shape, deviation, reach, cuts=(), kind=jnp.bfloat16):
    result = deviation * jax.random.normal(stream_key, shape, jnp.float32)
    if cuts:
        result = result * steps_of(stream_key, shape, cuts, -0.22, 0.18)
    return jnp.clip(result, -reach, reach).astype(kind)


def setup_inputs(seed: int = 0) -> dict:
    splits = jax.random.split(jax.random.key(seed), 11)
    queries = draw_queries(jax.random.fold_in(splits[10], 71), 0)
    keys = draw_keys(jax.random.fold_in(splits[10], 71), 0)
    values = centred(splits[2], (N_DP, LEN, KV_HEADS * HEAD_DIM), 1.0, 6.0, ((0, 4), (1, 4)))
    residual = centred(splits[3], (N_DP, LEN, D), 0.5, 4.0, ((0, 4), (1, 4)))
    labels = draw_labels(jax.random.fold_in(splits[10], 71), 0)
    block_mask = draw_block_mask(jax.random.fold_in(splits[10], 71), 0)
    gains = jnp.clip(1.0 + 0.1 * jax.random.normal(splits[6], (2, D), jnp.float32), 0.5, 1.5)
    w_gate = centred(splits[7], (D, 2 * FFW), D ** -0.5, 0.09375, ((1, 64),))
    w_up = centred(splits[8], (D, 2 * FFW), D ** -0.5, 0.09375, ((1, 64),))
    w_down = centred(splits[9], (2 * FFW, D), (FFW // 8) ** -0.5, 0.15625, ((0, 64),))
    return {"queries": queries, "keys": keys, "values": values, "residual": residual, "labels": labels, "block_mask": block_mask, "gains": gains, "w_gate": w_gate, "w_up": w_up, "w_down": w_down}


def one_sequence(queries, keys, values, residual, labels, block_mask, gains, w_gate, w_up, w_down):
    group = HEADS // KV_HEADS
    width = FFW
    positions = jnp.arange(LEN, dtype=jnp.int32)
    blocks = positions // BLOCK
    token_label = labels[blocks]
    allowed = block_mask[blocks][:, blocks] == 1
    same = blocks[:, None] == blocks[None, :]
    causal = positions[None, :] <= positions[:, None]
    visual = token_label == 1
    allowed = allowed & (jnp.logical_not(same) | causal | visual[:, None])
    q_heads = queries.astype(jnp.float32).reshape(LEN, KV_HEADS, group, HEAD_DIM)
    k_heads = keys.astype(jnp.float32).reshape(LEN, KV_HEADS, HEAD_DIM)
    v_heads = values.astype(jnp.float32).reshape(LEN, KV_HEADS, HEAD_DIM)
    scores = jnp.einsum('qgrd,kgd->grqk', q_heads, k_heads) / jnp.sqrt(jnp.float32(HEAD_DIM))
    scores = jnp.where(allowed[None, None], scores, -jnp.inf)
    top = lax.optimization_barrier(jnp.max(scores, axis=-1, keepdims=True))
    weights = jnp.where(allowed[None, None], jnp.exp(scores - top), 0.0)
    total = lax.optimization_barrier(jnp.sum(weights, axis=-1))
    soft = weights.astype(jnp.bfloat16).astype(jnp.float32)
    mixed = jnp.einsum('grqk,kgd->qgrd', soft, v_heads)
    mixed = mixed / jnp.transpose(total, (2, 0, 1))[..., None]
    attention = mixed.reshape(LEN, D).astype(jnp.bfloat16)
    mid = residual.astype(jnp.float32) + attention.astype(jnp.float32)
    gain_rows = jnp.where(visual[:, None], gains[1][None, :], gains[0][None, :])
    normed = (mid * lax.rsqrt(lax.optimization_barrier(jnp.mean(mid * mid, axis=-1, keepdims=True)) + 1e-05) * gain_rows).astype(jnp.bfloat16)
    branch = jnp.zeros((LEN, D), jnp.float32)
    for modality in range(2):
        gate = jnp.dot(normed, w_gate[:, modality * width:(modality + 1) * width], preferred_element_type=jnp.float32)
        upper = jnp.dot(normed, w_up[:, modality * width:(modality + 1) * width], preferred_element_type=jnp.float32)
        hidden = (jax.nn.silu(gate) * upper).astype(jnp.bfloat16)
        part = jnp.dot(hidden, w_down[modality * width:(modality + 1) * width], preferred_element_type=jnp.float32)
        branch = branch + jnp.where((token_label == modality)[:, None], part, 0.0)
    return (mid + branch).astype(jnp.bfloat16)

def reference(queries, keys, values, residual, labels, block_mask, gains, w_gate, w_up, w_down):

    def single(index):
        return one_sequence(queries[index], keys[index], values[index], residual[index], labels[index], block_mask[index], gains, w_gate, w_up, w_down)
    return lax.map(single, jnp.arange(N_DP, dtype=jnp.int32))
```

```python
import functools
import math

import jax
import jax.numpy as jnp
from jax import lax
from jax.experimental import pallas as pl
from jax.experimental.pallas import tpu as pltpu
from jax.sharding import PartitionSpec as P

KV_HEADS = 4
HEAD_DIM = 128
BLOCK = 128
NEG = -1e30
MESH = pl.DeviceIdType.MESH
PIECES = 2
STREAMS = 2
ANY = pl.BlockSpec(memory_space=pl.ANY)
VMEM = pl.BlockSpec(memory_space=pltpu.VMEM)
SMEM = pl.BlockSpec(memory_space=pltpu.SMEM)


def kv_kernel(k_ref, v_ref, ko_ref, vo_ref, lsem, ssem, rsem):
    rows = k_ref.shape[0]
    piece = rows // PIECES
    c = lax.axis_index("ctx")
    e = lax.axis_index("exp")
    sib = c + 1 - 2 * (c % 2)
    oth = (c + 2) % 4
    twin = e + 1 - 2 * (e % 2)
    barrier = pltpu.get_barrier_semaphore()
    for dev in ({"ctx": sib}, {"ctx": oth}, {"ctx": oth, "exp": twin}):
        pl.semaphore_signal(barrier, inc=1, device_id=dev, device_id_type=MESH)
    pl.semaphore_wait(barrier, 3)

    def rows_at(shard, i, size):
        return pl.ds(pl.multiple_of(shard * rows + i * size, size), size)

    cross, started = [], []
    for i in range(PIECES):
        for kind, (src, dst, dev) in enumerate(
            ((k_ref, ko_ref, {"ctx": oth}), (v_ref, vo_ref, {"ctx": oth, "exp": twin}))
        ):
            copy = pltpu.make_async_remote_copy(
                src_ref=src.at[pl.ds(i * piece, piece)],
                dst_ref=dst.at[rows_at(c, i, piece)],
                send_sem=ssem.at[kind, i],
                recv_sem=rsem.at[kind, i],
                device_id=dev,
                device_id_type=MESH,
            )
            copy.start()
            cross.append(copy)
    for kind, (src, dst) in enumerate(((k_ref, ko_ref), (v_ref, vo_ref))):
        copy = pltpu.make_async_remote_copy(
            src_ref=src,
            dst_ref=dst.at[rows_at(c, 0, rows)],
            send_sem=ssem.at[2 + kind, 0],
            recv_sem=rsem.at[2 + kind, 0],
            device_id={"ctx": sib},
            device_id_type=MESH,
        )
        copy.start()
        started.append(copy)
    local = []
    for kind, (src, dst) in enumerate(((k_ref, ko_ref), (v_ref, vo_ref))):
        copy = pltpu.make_async_copy(src, dst.at[rows_at(c, 0, rows)], lsem.at[kind])
        copy.start()
        local.append(copy)
    for i in range(PIECES):
        for kind, dst in enumerate((ko_ref, vo_ref)):
            cross[2 * i + kind].wait_recv()
            copy = pltpu.make_async_remote_copy(
                src_ref=dst.at[rows_at(oth, i, piece)],
                dst_ref=dst.at[rows_at(oth, i, piece)],
                send_sem=ssem.at[4 + kind, i],
                recv_sem=rsem.at[4 + kind, i],
                device_id={"ctx": sib},
                device_id_type=MESH,
            )
            copy.start()
            started.append(copy)
    for copy in started:
        copy.wait_recv()
    for copy in cross + started:
        copy.wait_send()
    for copy in local:
        copy.wait()


def kv_exchange(keys, values):
    rows, width = keys.shape
    whole = jax.ShapeDtypeStruct((4 * rows, width), keys.dtype)
    return pl.pallas_call(
        kv_kernel,
        out_shape=(whole, whole),
        in_specs=[ANY, ANY],
        out_specs=(ANY, ANY),
        scratch_shapes=[
            pltpu.SemaphoreType.DMA((2,)),
            pltpu.SemaphoreType.DMA((6, PIECES)),
            pltpu.SemaphoreType.DMA((6, PIECES)),
        ],
        compiler_params=pltpu.CompilerParams(collective_id=0, has_side_effects=True),
        name="kv_exchange",
    )(keys, values)


def layer_kernel(
    label_ref, mask_ref, q_ref, k_ref, v_ref, res_ref, gain_ref, wg_any, wu_any, wd_any,
    part_ref, own_ref, bias, mid, normed, wg, wu, wd, sems,
):
    rows, width = q_ref.shape
    count = k_ref.shape[0]
    heads = width // HEAD_DIM
    group = heads // KV_HEADS
    here = rows // BLOCK
    copies = [
        pltpu.make_async_copy(src, dst, sems.at[i])
        for i, (src, dst) in enumerate(((wg_any, wg), (wu_any, wu), (wd_any, wd)))
    ]
    for copy in copies:
        copy.start()
    first = lax.axis_index("ctx") * here
    e = lax.axis_index("exp")
    exp_count = lax.axis_size("exp")
    causal = lax.broadcasted_iota(jnp.int32, (BLOCK, BLOCK), 1) <= lax.broadcasted_iota(
        jnp.int32, (BLOCK, BLOCK), 0
    )
    for b in range(here):
        q_blk = first + b
        for j in range(count // BLOCK):
            sees = mask_ref[q_blk, j] == 1
            whole = sees & ((q_blk != j) | (label_ref[q_blk] == 1))
            upper = jnp.where(whole, 0.0, NEG)
            lower = jnp.where(sees, 0.0, NEG)
            bias[b * BLOCK:(b + 1) * BLOCK, j * BLOCK:(j + 1) * BLOCK] = jnp.where(causal, lower, upper)
    factor = math.log2(math.e) / math.sqrt(HEAD_DIM)

    def head(h, squares):
        at = pl.ds(pl.multiple_of(h * HEAD_DIM, HEAD_DIM), HEAD_DIM)
        kv_at = pl.ds(pl.multiple_of((h // group) * HEAD_DIM, HEAD_DIM), HEAD_DIM)
        scores = lax.dot_general(
            q_ref[:, at], k_ref[:, kv_at], (((1,), (1,)), ((), ())), preferred_element_type=jnp.float32
        ) + bias[...]
        top = jnp.max(scores, axis=-1, keepdims=True)
        weights = jnp.exp2((scores - top) * factor)
        total = jnp.sum(weights, axis=-1, keepdims=True)
        mixed = jnp.dot(weights.astype(jnp.bfloat16), v_ref[:, kv_at], preferred_element_type=jnp.float32)
        x = res_ref[:, at].astype(jnp.float32) + (mixed / total).astype(jnp.bfloat16).astype(jnp.float32)
        mid[:, at] = x
        return squares + x * x

    squares = lax.fori_loop(0, heads, head, jnp.zeros((rows, HEAD_DIM), jnp.float32))
    inverse = lax.rsqrt(jnp.sum(squares, axis=-1, keepdims=True) / width + 1e-05)
    for b in range(here):
        at = slice(b * BLOCK, (b + 1) * BLOCK)
        visual = label_ref[first + b] == 1
        gain = jnp.where(visual, gain_ref[1:2, :], gain_ref[0:1, :])
        normed[at, :] = (mid[at, :] * inverse[at] * gain).astype(jnp.bfloat16)
    slot = rows // (exp_count // 2)
    own_ref[...] = mid[pl.ds(pl.multiple_of((e // 2) * slot, slot), slot), :]
    for copy in copies:
        copy.wait()
    x = normed[...]
    last = (((1,), (1,)), ((), ()))
    gate = lax.dot_general(x, wg[...], last, preferred_element_type=jnp.float32)
    upper = lax.dot_general(x, wu[...], last, preferred_element_type=jnp.float32)
    hidden = (jax.nn.silu(gate) * upper).astype(jnp.bfloat16)
    section = jnp.where(e >= exp_count // 2, 1, 0)
    tile = 512
    for t in range(width // tile):
        cols = slice(t * tile, (t + 1) * tile)
        out = jnp.dot(hidden, wd[:, cols], preferred_element_type=jnp.float32)
        for b in range(here):
            keep = label_ref[first + b] == section
            kept = jnp.where(keep, out[b * BLOCK:(b + 1) * BLOCK], 0.0)
            part_ref[b * (BLOCK // slot):(b + 1) * (BLOCK // slot), :, cols] = kept.reshape(
                BLOCK // slot, slot, tile
            ).astype(jnp.bfloat16)


def layer(labels, mask, q, k, v, res, gains, wg, wu, wd, exp_count):
    rows, width = q.shape
    hidden = wg.shape[0]
    slots = exp_count // 2
    slot = rows // slots
    return pl.pallas_call(
        layer_kernel,
        out_shape=(
            jax.ShapeDtypeStruct((slots, slot, width), jnp.bfloat16),
            jax.ShapeDtypeStruct((slot, width), jnp.float32),
        ),
        in_specs=[SMEM, SMEM, VMEM, VMEM, VMEM, VMEM, VMEM, ANY, ANY, ANY],
        out_specs=(VMEM, VMEM),
        scratch_shapes=[
            pltpu.VMEM((rows, k.shape[0]), jnp.float32),
            pltpu.VMEM((rows, width), jnp.float32),
            pltpu.VMEM((rows, width), jnp.bfloat16),
            pltpu.VMEM((hidden, width), jnp.bfloat16),
            pltpu.VMEM((hidden, width), jnp.bfloat16),
            pltpu.VMEM((hidden, width), jnp.bfloat16),
            pltpu.SemaphoreType.DMA((3,)),
        ],
        compiler_params=pltpu.CompilerParams(vmem_limit_bytes=48 * 1024 * 1024),
        name="layer",
    )(labels, mask, q, k, v, res, gains, wg, wu, wd)


def reduce_kernel(slots, part_ref, mid_ref, out_ref, up_buf, dn_buf, tw_in, tw_out, ssem, rsem, tsem):
    width = part_ref.shape[2]
    cols = width // STREAMS
    half = slots // 2
    e = lax.axis_index("exp")
    z = e // 2
    count = 2 * slots
    up = (e + 2) % count
    dn = (e + count - 2) % count
    twin = e + 1 - 2 * (e % 2)
    barrier = pltpu.get_barrier_semaphore()
    for dev in (up, dn, twin):
        pl.semaphore_signal(barrier, inc=1, device_id={"exp": dev}, device_id_type=MESH)
    pl.semaphore_wait(barrier, 3)

    def hop(way, src, step, t):
        buf = (up_buf, dn_buf)[way]
        return pltpu.make_async_remote_copy(
            src_ref=src,
            dst_ref=buf.at[step, :, pl.ds(t * cols, cols)],
            send_sem=ssem.at[way, step, t],
            recv_sem=rsem.at[way, step, t],
            device_id={"exp": (up, dn)[way]},
            device_id_type=MESH,
        )

    def slot_of(way, step):
        if way == 0:
            return (z + half - 1 - step + slots) % slots
        return (z + half + step) % slots

    for t in range(STREAMS):
        for way in range(2):
            hop(way, part_ref.at[slot_of(way, 0), :, pl.ds(t * cols, cols)], 0, t).start()

    def advance(way, step, t):
        buf = (up_buf, dn_buf)[way]
        at = pl.ds(t * cols, cols)
        src = buf.at[step - 1, :, at]
        hop(way, src, step - 1, t).wait_recv()
        own = part_ref[slot_of(way, step), :, at]
        buf[step - 1, :, at] = (buf[step - 1, :, at].astype(jnp.float32) + own.astype(jnp.float32)).astype(
            jnp.bfloat16
        )
        hop(way, src, step, t).start()

    def both(step, carry):
        for t in range(STREAMS):
            for way in range(2):
                advance(way, step, t)
        return carry

    lax.fori_loop(1, half - 1, both, 0)
    for t in range(STREAMS):
        advance(1, half - 1, t)
    for t in range(STREAMS):
        at = pl.ds(t * cols, cols)
        hop(0, up_buf.at[half - 2, :, at], half - 2, t).wait_recv()
        hop(1, dn_buf.at[half - 1, :, at], half - 1, t).wait_recv()
    mine = (
        part_ref[z].astype(jnp.float32)
        + up_buf[half - 2].astype(jnp.float32)
        + dn_buf[half - 1].astype(jnp.float32)
    )
    tw_out[...] = mine.astype(jnp.bfloat16)
    swap = pltpu.make_async_remote_copy(
        src_ref=tw_out, dst_ref=tw_in, send_sem=tsem.at[0], recv_sem=tsem.at[1],
        device_id={"exp": twin}, device_id_type=MESH,
    )
    swap.start()
    swap.wait_recv()
    total = mid_ref[...] + (mine + tw_in[...].astype(jnp.float32))
    size = total.shape[0] // 2
    picked = jnp.where(e % 2 == 0, total[:size], total[size:])
    out_ref[...] = picked.astype(jnp.bfloat16)
    swap.wait_send()

    def drain(step, carry):
        for t in range(STREAMS):
            for way in range(2):
                hop(way, part_ref.at[0, :, pl.ds(t * cols, cols)], step, t).wait_send()
        return carry

    lax.fori_loop(0, half - 1, drain, 0)
    for t in range(STREAMS):
        hop(1, part_ref.at[0, :, pl.ds(t * cols, cols)], half - 1, t).wait_send()


def reduce_parts(part, mid):
    slots, slot, width = part.shape
    half = slots // 2
    return pl.pallas_call(
        functools.partial(reduce_kernel, slots),
        out_shape=jax.ShapeDtypeStruct((slot // 2, width), jnp.bfloat16),
        in_specs=[VMEM, VMEM],
        out_specs=VMEM,
        scratch_shapes=[
            pltpu.VMEM((half, slot, width), jnp.bfloat16),
            pltpu.VMEM((half, slot, width), jnp.bfloat16),
            pltpu.VMEM((slot, width), jnp.bfloat16),
            pltpu.VMEM((slot, width), jnp.bfloat16),
            pltpu.SemaphoreType.DMA((2, half, STREAMS)),
            pltpu.SemaphoreType.DMA((2, half, STREAMS)),
            pltpu.SemaphoreType.DMA((2,)),
        ],
        compiler_params=pltpu.CompilerParams(collective_id=1, has_side_effects=True),
        name="reduce_parts",
    )(part, mid)


def per_device(queries, keys, values, residual, labels, block_mask, gains, w_gate, w_up, w_down):
    whole_keys, whole_values = kv_exchange(keys[0], values[0])
    part, own = layer(
        labels[0], block_mask[0], queries[0], whole_keys, whole_values, residual[0], gains,
        w_gate.T, w_up.T, w_down, lax.axis_size("exp"),
    )
    return reduce_parts(part, own)[None]


def solution(mesh):
    placed = (
        P("dp", "ctx", None),
        P("dp", "ctx", None),
        P("dp", "ctx", None),
        P("dp", "ctx", None),
        P("dp", None),
        P("dp", None, None),
        P(),
        P(None, "exp"),
        P(None, "exp"),
        P("exp", None),
    )
    return jax.shard_map(
        per_device,
        mesh=mesh,
        in_specs=placed,
        out_specs=P("dp", ("ctx", "exp"), None),
        check_vma=False,
    )
```

```python
import functools
import math

import jax
import jax.numpy as jnp
from jax import lax
from jax.experimental import pallas as pl
from jax.experimental.pallas import tpu as pltpu
from jax.sharding import PartitionSpec as P

KV_HEADS = 4
HEAD_DIM = 128
BLOCK = 128
NEG = -1e30
MESH = pl.DeviceIdType.MESH
PIECES = 2
STREAMS = 4
ANY = pl.BlockSpec(memory_space=pl.ANY)
VMEM = pl.BlockSpec(memory_space=pltpu.VMEM)
SMEM = pl.BlockSpec(memory_space=pltpu.SMEM)


def kv_kernel(k_ref, v_ref, ko_ref, vo_ref, lsem, ssem, rsem):
    rows = k_ref.shape[0]
    piece = rows // PIECES
    c = lax.axis_index("ctx")
    e = lax.axis_index("exp")
    sib = c + 1 - 2 * (c % 2)
    oth = (c + 2) % 4
    twin = e + 1 - 2 * (e % 2)
    barrier = pltpu.get_barrier_semaphore()
    for dev in ({"ctx": sib}, {"ctx": oth}, {"ctx": oth, "exp": twin}):
        pl.semaphore_signal(barrier, inc=1, device_id=dev, device_id_type=MESH)
    pl.semaphore_wait(barrier, 3)

    def rows_at(shard, i, size):
        return pl.ds(pl.multiple_of(shard * rows + i * size, size), size)

    cross, started = [], []
    for i in range(PIECES):
        for kind, (src, dst, dev) in enumerate(
            ((k_ref, ko_ref, {"ctx": oth}), (v_ref, vo_ref, {"ctx": oth, "exp": twin}))
        ):
            copy = pltpu.make_async_remote_copy(
                src_ref=src.at[pl.ds(i * piece, piece)],
                dst_ref=dst.at[rows_at(c, i, piece)],
                send_sem=ssem.at[kind, i],
                recv_sem=rsem.at[kind, i],
                device_id=dev,
                device_id_type=MESH,
            )
            copy.start()
            cross.append(copy)
    for kind, (src, dst) in enumerate(((k_ref, ko_ref), (v_ref, vo_ref))):
        copy = pltpu.make_async_remote_copy(
            src_ref=src,
            dst_ref=dst.at[rows_at(c, 0, rows)],
            send_sem=ssem.at[2 + kind, 0],
            recv_sem=rsem.at[2 + kind, 0],
            device_id={"ctx": sib},
            device_id_type=MESH,
        )
        copy.start()
        started.append(copy)
    local = []
    for kind, (src, dst) in enumerate(((k_ref, ko_ref), (v_ref, vo_ref))):
        copy = pltpu.make_async_copy(src, dst.at[rows_at(c, 0, rows)], lsem.at[kind])
        copy.start()
        local.append(copy)
    for i in range(PIECES):
        for kind, dst in enumerate((ko_ref, vo_ref)):
            cross[2 * i + kind].wait_recv()
            copy = pltpu.make_async_remote_copy(
                src_ref=dst.at[rows_at(oth, i, piece)],
                dst_ref=dst.at[rows_at(oth, i, piece)],
                send_sem=ssem.at[4 + kind, i],
                recv_sem=rsem.at[4 + kind, i],
                device_id={"ctx": sib},
                device_id_type=MESH,
            )
            copy.start()
            started.append(copy)
    for copy in started:
        copy.wait_recv()
    for copy in cross + started:
        copy.wait_send()
    for copy in local:
        copy.wait()


def kv_exchange(keys, values):
    rows, width = keys.shape
    whole = jax.ShapeDtypeStruct((4 * rows, width), keys.dtype)
    return pl.pallas_call(
        kv_kernel,
        out_shape=(whole, whole),
        in_specs=[ANY, ANY],
        out_specs=(ANY, ANY),
        scratch_shapes=[
            pltpu.SemaphoreType.DMA((2,)),
            pltpu.SemaphoreType.DMA((6, PIECES)),
            pltpu.SemaphoreType.DMA((6, PIECES)),
        ],
        compiler_params=pltpu.CompilerParams(collective_id=0, has_side_effects=True),
        name="kv_exchange",
    )(keys, values)


def chains(slots):
    half = slots // 2
    near = half // 2
    return ((1, half - 1, near + 1), (-1, half, near + 1), (1, near, 1), (-1, near, 1))


def layer_kernel(
    slots, label_ref, mask_ref, gain_ref, q_any, k_any, v_any, res_any, wg_any, wu_any, wd_any,
    out_ref, q_ref, k_ref, v_ref, res_ref, bias, mid, normed, wg, wu, wd, part,
    buf, fin, tw_in, tw_out, lsem, ssem, rsem, tsem,
):
    rows, width = q_ref.shape
    count = k_ref.shape[0]
    heads = width // HEAD_DIM
    group = heads // KV_HEADS
    here = rows // BLOCK
    slot = rows // slots
    cols = width // STREAMS
    first = lax.axis_index("ctx") * here
    e = lax.axis_index("exp")
    z = e // 2
    twin = e + 1 - 2 * (e % 2)
    plan = chains(slots)
    reach = plan[0][2]

    def along(distance):
        return (e + 2 * (distance + slots)) % (2 * slots)

    barrier = pltpu.get_barrier_semaphore()
    partners = [along(1), along(-1), along(reach), along(-reach), twin]
    for dev in partners:
        pl.semaphore_signal(barrier, inc=1, device_id={"exp": dev}, device_id_type=MESH)
    loads = [
        pltpu.make_async_copy(src, dst, lsem.at[i])
        for i, (src, dst) in enumerate(
            (
                (q_any, q_ref), (k_any, k_ref), (v_any, v_ref), (res_any, res_ref),
                (wg_any, wg), (wu_any, wu), (wd_any, wd),
            )
        )
    ]
    for load in loads:
        load.start()
    causal = lax.broadcasted_iota(jnp.int32, (BLOCK, BLOCK), 1) <= lax.broadcasted_iota(
        jnp.int32, (BLOCK, BLOCK), 0
    )
    for b in range(here):
        q_blk = first + b
        for j in range(count // BLOCK):
            sees = mask_ref[q_blk, j] == 1
            whole = sees & ((q_blk != j) | (label_ref[q_blk] == 1))
            upper = jnp.where(whole, 0.0, NEG)
            lower = jnp.where(sees, 0.0, NEG)
            bias[b * BLOCK:(b + 1) * BLOCK, j * BLOCK:(j + 1) * BLOCK] = jnp.where(causal, lower, upper)
    for load in loads[:4]:
        load.wait()
    factor = math.log2(math.e) / math.sqrt(HEAD_DIM)

    def head(h, squares):
        at = pl.ds(pl.multiple_of(h * HEAD_DIM, HEAD_DIM), HEAD_DIM)
        kv_at = pl.ds(pl.multiple_of((h // group) * HEAD_DIM, HEAD_DIM), HEAD_DIM)
        scores = lax.dot_general(
            q_ref[:, at], k_ref[:, kv_at], (((1,), (1,)), ((), ())), preferred_element_type=jnp.float32
        ) + bias[...]
        top = jnp.max(scores, axis=-1, keepdims=True)
        weights = jnp.exp2((scores - top) * factor)
        total = jnp.sum(weights, axis=-1, keepdims=True)
        mixed = jnp.dot(weights.astype(jnp.bfloat16), v_ref[:, kv_at], preferred_element_type=jnp.float32)
        x = res_ref[:, at].astype(jnp.float32) + (mixed / total).astype(jnp.bfloat16).astype(jnp.float32)
        mid[:, at] = x
        return squares + x * x

    squares = lax.fori_loop(0, heads, head, jnp.zeros((rows, HEAD_DIM), jnp.float32))
    inverse = lax.rsqrt(jnp.sum(squares, axis=-1, keepdims=True) / width + 1e-05)
    for b in range(here):
        at = slice(b * BLOCK, (b + 1) * BLOCK)
        visual = label_ref[first + b] == 1
        gain = jnp.where(visual, gain_ref[1:2, :], gain_ref[0:1, :])
        normed[at, :] = (mid[at, :] * inverse[at] * gain).astype(jnp.bfloat16)
    for load in loads[4:]:
        load.wait()
    x = normed[...]
    last = (((1,), (1,)), ((), ()))
    gate = lax.dot_general(x, wg[...], last, preferred_element_type=jnp.float32)
    upper = lax.dot_general(x, wu[...], last, preferred_element_type=jnp.float32)
    hidden = (jax.nn.silu(gate) * upper).astype(jnp.bfloat16)
    pl.semaphore_wait(barrier, len(partners))

    def hop(i, step, t, src):
        way, farthest, nearest = plan[i]
        final = isinstance(step, int) and step == farthest - nearest
        at = pl.ds(t * cols, cols)
        return pltpu.make_async_remote_copy(
            src_ref=src,
            dst_ref=fin.at[i, :, at] if final else buf.at[i, step, :, at],
            send_sem=ssem.at[i, step, t],
            recv_sem=rsem.at[i, step, t],
            device_id={"exp": along(way * nearest if final else way)},
            device_id_type=MESH,
        )

    def chunk(i, step):
        way, farthest, _ = plan[i]
        return (z + way * (farthest - step) + 2 * slots) % slots

    def advance(i, step, t):
        at = pl.ds(t * cols, cols)
        src = buf.at[i, step - 1, :, at]
        hop(i, step - 1, t, src).wait_recv()
        own = part[chunk(i, step), :, at]
        buf[i, step - 1, :, at] = (buf[i, step - 1, :, at].astype(jnp.float32) + own.astype(jnp.float32)).astype(
            jnp.bfloat16
        )
        hop(i, step, t, src).start()

    section = jnp.where(e >= slots, 1, 0)
    tile = width // 4
    for u in range(4):
        span = slice(u * tile, (u + 1) * tile)
        out = jnp.dot(hidden, wd[:, span], preferred_element_type=jnp.float32)
        for b in range(here):
            keep = label_ref[first + b] == section
            kept = jnp.where(keep, out[b * BLOCK:(b + 1) * BLOCK], 0.0)
            part[b * (BLOCK // slot):(b + 1) * (BLOCK // slot), :, span] = kept.reshape(
                BLOCK // slot, slot, tile
            ).astype(jnp.bfloat16)
        for t in range(STREAMS):
            if (u + 1) * STREAMS == 4 * (t + 1):
                for i in range(len(plan)):
                    hop(i, 0, t, part.at[chunk(i, 0), :, pl.ds(t * cols, cols)]).start()

    lengths = [farthest - nearest + 1 for _, farthest, nearest in plan]
    same = min(lengths) - 1

    def step_all(step, carry):
        for t in range(STREAMS):
            for i in range(len(plan)):
                advance(i, step, t)
        return carry

    if same > 1:
        lax.fori_loop(1, same, step_all, 0)
    for step in range(max(same, 1), max(lengths)):
        for t in range(STREAMS):
            for i in range(len(plan)):
                if step < lengths[i]:
                    advance(i, step, t)
    mine = part[z].astype(jnp.float32)
    for i in (2, 3, 0, 1):
        for t in range(STREAMS):
            at = pl.ds(t * cols, cols)
            hop(i, lengths[i] - 1, t, fin.at[i, :, at]).wait_recv()
        mine = mine + fin[i].astype(jnp.float32)
    tw_out[...] = mine.astype(jnp.bfloat16)
    swap = pltpu.make_async_remote_copy(
        src_ref=tw_out, dst_ref=tw_in, send_sem=tsem.at[0], recv_sem=tsem.at[1],
        device_id={"exp": twin}, device_id_type=MESH,
    )
    swap.start()
    swap.wait_recv()
    total = mid[pl.ds(pl.multiple_of(z * slot, slot), slot), :] + (mine + tw_in[...].astype(jnp.float32))
    size = slot // 2
    out_ref[...] = jnp.where(e % 2 == 0, total[:size], total[size:]).astype(jnp.bfloat16)
    swap.wait_send()
    for i in range(len(plan)):
        for step in range(lengths[i]):
            for t in range(STREAMS):
                hop(i, step, t, part.at[0, :, pl.ds(t * cols, cols)]).wait_send()


def layer(labels, mask, q, k, v, res, gains, wg, wu, wd, exp_count):
    rows, width = q.shape
    hidden = wg.shape[0]
    slots = exp_count // 2
    slot = rows // slots
    steps = slots // 4
    half = jnp.bfloat16
    return pl.pallas_call(
        functools.partial(layer_kernel, slots),
        out_shape=jax.ShapeDtypeStruct((slot // 2, width), half),
        in_specs=[SMEM, SMEM, VMEM, ANY, ANY, ANY, ANY, ANY, ANY, ANY],
        out_specs=VMEM,
        scratch_shapes=[
            pltpu.VMEM((rows, width), half),
            pltpu.VMEM(k.shape, half),
            pltpu.VMEM(v.shape, half),
            pltpu.VMEM((rows, width), half),
            pltpu.VMEM((rows, k.shape[0]), jnp.float32),
            pltpu.VMEM((rows, width), jnp.float32),
            pltpu.VMEM((rows, width), half),
            pltpu.VMEM((hidden, width), half),
            pltpu.VMEM((hidden, width), half),
            pltpu.VMEM((hidden, width), half),
            pltpu.VMEM((slots, slot, width), half),
            pltpu.VMEM((4, steps, slot, width), half),
            pltpu.VMEM((4, slot, width), half),
            pltpu.VMEM((slot, width), half),
            pltpu.VMEM((slot, width), half),
            pltpu.SemaphoreType.DMA((7,)),
            pltpu.SemaphoreType.DMA((4, steps, STREAMS)),
            pltpu.SemaphoreType.DMA((4, steps, STREAMS)),
            pltpu.SemaphoreType.DMA((2,)),
        ],
        compiler_params=pltpu.CompilerParams(
            vmem_limit_bytes=58 * 1024 * 1024, collective_id=1, has_side_effects=True
        ),
        name="layer",
    )(labels, mask, gains, q, k, v, res, wg, wu, wd)


def per_device(queries, keys, values, residual, labels, block_mask, gains, w_gate, w_up, w_down):
    whole_keys, whole_values = kv_exchange(keys[0], values[0])
    out = layer(
        labels[0], block_mask[0], queries[0], whole_keys, whole_values, residual[0], gains,
        w_gate.T, w_up.T, w_down, lax.axis_size("exp"),
    )
    return out[None]


def solution(mesh):
    placed = (
        P("dp", "ctx", None),
        P("dp", "ctx", None),
        P("dp", "ctx", None),
        P("dp", "ctx", None),
        P("dp", None),
        P("dp", None, None),
        P(),
        P(None, "exp"),
        P(None, "exp"),
        P("exp", None),
    )
    return jax.shard_map(
        per_device,
        mesh=mesh,
        in_specs=placed,
        out_specs=P("dp", ("ctx", "exp"), None),
        check_vma=False,
    )
```

```python
import functools
import math

import jax
import jax.numpy as jnp
from jax import lax
from jax.experimental import pallas as pl
from jax.experimental.pallas import tpu as pltpu
from jax.sharding import PartitionSpec as P

KV_HEADS = 4
HEAD_DIM = 128
BLOCK = 128
NEG = -1e30
MESH = pl.DeviceIdType.MESH
STREAMS = 4
ANY = pl.BlockSpec(memory_space=pl.ANY)
VMEM = pl.BlockSpec(memory_space=pltpu.VMEM)
SMEM = pl.BlockSpec(memory_space=pltpu.SMEM)


def chains(slots):
    half = slots // 2
    near = half // 2
    return ((1, half - 1, near + 1), (-1, half, near + 1), (1, near, 1), (-1, near, 1))


def layer_kernel(
    slots, label_ref, mask_ref, gain_ref, q_any, k_any, v_any, res_any, wg_any, wu_any, wd_any,
    out_ref, q_ref, kv_ref, res_ref, bias, tops, sums, mid, normed, wg, wu, wd, part,
    buf, fin, tw_in, tw_out, lsem, ksem, kssem, krsem, ssem, rsem, tsem, known,
):
    rows, width = q_ref.shape
    count = kv_ref.shape[2]
    heads = width // HEAD_DIM
    group = heads // KV_HEADS
    here = rows // BLOCK
    slot = rows // slots
    cols = width // STREAMS
    c = lax.axis_index("ctx")
    first = c * here
    e = lax.axis_index("exp")
    z = e // 2
    twin = e + 1 - 2 * (e % 2)
    sib = c + 1 - 2 * (c % 2)
    oth = (c + 2) % 4
    plan = chains(slots)
    reach = plan[0][2]

    def along(distance):
        return (e + 2 * (distance + slots)) % (2 * slots)

    barrier = pltpu.get_barrier_semaphore()
    partners = [{"exp": along(1)}, {"exp": along(-1)}, {"exp": twin}, {"ctx": sib}, {"ctx": oth}]
    partners.append({"ctx": oth, "exp": twin})
    for dev in partners:
        pl.semaphore_signal(barrier, inc=1, device_id=dev, device_id_type=MESH)
    own_loads = [
        pltpu.make_async_copy(
            src.at[:, pl.ds(g * HEAD_DIM, HEAD_DIM)], kv_ref.at[kind, g, pl.ds(0, rows)], ksem.at[kind, g]
        )
        for g in range(KV_HEADS)
        for kind, src in enumerate((k_any, v_any))
    ]
    loads = [
        pltpu.make_async_copy(src, dst, lsem.at[i])
        for i, (src, dst) in enumerate(
            ((q_any, q_ref), (res_any, res_ref), (wg_any, wg), (wu_any, wu), (wd_any, wd))
        )
    ]
    for load in own_loads + loads:
        load.start()
    causal = lax.broadcasted_iota(jnp.int32, (BLOCK, BLOCK), 1) <= lax.broadcasted_iota(
        jnp.int32, (BLOCK, BLOCK), 0
    )
    for b in range(here):
        q_blk = first + b
        for r, shard in enumerate((c, sib, oth, sib + 2 - 4 * (sib // 2))):
            for j in range(here):
                sees = mask_ref[q_blk, shard * here + j] == 1
                lower = jnp.where(sees, 0.0, NEG)
                if r == 0 and j == b:
                    upper = jnp.where(sees & (label_ref[q_blk] == 1), 0.0, NEG)
                    square = jnp.where(causal, lower, upper)
                else:
                    square = jnp.full((BLOCK, BLOCK), lower, jnp.float32)
                at = r * rows + j * BLOCK
                bias[b * BLOCK:(b + 1) * BLOCK, at:at + BLOCK] = square
    for load in own_loads:
        load.wait()

    def piece(stage, kind, g):
        source, target, dev = (
            (0, 2, {"ctx": oth, "exp": twin} if kind else {"ctx": oth}),
            (0, 1, {"ctx": sib}),
            (2, 3, {"ctx": sib}),
        )[stage]
        return pltpu.make_async_remote_copy(
            src_ref=kv_ref.at[kind, g, pl.ds(source * rows, rows)],
            dst_ref=kv_ref.at[kind, g, pl.ds(target * rows, rows)],
            send_sem=kssem.at[stage, kind, g],
            recv_sem=krsem.at[stage, kind, g],
            device_id=dev,
            device_id_type=MESH,
        )

    pl.semaphore_wait(barrier, len(partners))
    for stage in range(2):
        for g in range(KV_HEADS):
            for kind in range(2):
                piece(stage, kind, g).start()

    def tell(i, distance):
        for way in (distance, -distance):
            pl.semaphore_signal(known.at[i], inc=1, device_id={"exp": along(way)}, device_id_type=MESH)

    def learn(i):
        pl.semaphore_wait(known.at[i], 2)

    hops = [1]
    distance = 2
    while distance * 2 <= reach:
        hops.append(distance)
        distance *= 2
    hops += [1] * (reach - distance)
    tell(0, hops[0])
    for load in loads[:2]:
        load.wait()
    factor = math.log2(math.e) / math.sqrt(HEAD_DIM)

    def place(h):
        return pl.ds(pl.multiple_of(h * HEAD_DIM, HEAD_DIM), HEAD_DIM)

    def scores_of(h, g, span):
        return lax.dot_general(
            q_ref[:, place(h)], kv_ref[0, g, span], (((1,), (1,)), ((), ())), preferred_element_type=jnp.float32
        ) + bias[:, span]

    def begin(h, carry):
        g = h // group
        scores = scores_of(h, g, slice(0, rows))
        top = jnp.max(scores, axis=-1, keepdims=True)
        weights = jnp.exp2((scores - top) * factor)
        tops[h] = top
        sums[h] = jnp.sum(weights, axis=-1, keepdims=True)
        mid[:, place(h)] = jnp.dot(
            weights.astype(jnp.bfloat16), kv_ref[1, g, 0:rows], preferred_element_type=jnp.float32
        )
        return carry

    lax.fori_loop(0, heads, begin, 0)

    def finish(g, h, squares):
        rest = slice(rows, count)
        scores = scores_of(h, g, rest)
        old = tops[h]
        top = jnp.maximum(old, jnp.max(scores, axis=-1, keepdims=True))
        weights = jnp.exp2((scores - top) * factor)
        shrink = jnp.exp2((old - top) * factor)
        total = sums[h] * shrink + jnp.sum(weights, axis=-1, keepdims=True)
        mixed = mid[:, place(h)] * shrink + jnp.dot(
            weights.astype(jnp.bfloat16), kv_ref[1, g, rest], preferred_element_type=jnp.float32
        )
        x = res_ref[:, place(h)].astype(jnp.float32) + (mixed / total).astype(jnp.bfloat16).astype(jnp.float32)
        mid[:, place(h)] = x
        return squares + x * x

    def forward(g):
        for kind in range(2):
            piece(0, kind, g).wait_recv()
            piece(2, kind, g).start()

    forward(0)
    squares = jnp.zeros((rows, HEAD_DIM), jnp.float32)
    for g in range(KV_HEADS):
        if g + 1 < KV_HEADS:
            forward(g + 1)
        for stage in (1, 2):
            for kind in range(2):
                piece(stage, kind, g).wait_recv()
        if g < len(hops):
            learn(g)
            if g + 1 < len(hops):
                tell(g + 1, hops[g + 1])
        squares = lax.fori_loop(g * group, (g + 1) * group, functools.partial(finish, g), squares)
    inverse = lax.rsqrt(jnp.sum(squares, axis=-1, keepdims=True) / width + 1e-05)
    for b in range(here):
        at = slice(b * BLOCK, (b + 1) * BLOCK)
        visual = label_ref[first + b] == 1
        gain = jnp.where(visual, gain_ref[1:2, :], gain_ref[0:1, :])
        normed[at, :] = (mid[at, :] * inverse[at] * gain).astype(jnp.bfloat16)
    for load in loads[2:]:
        load.wait()
    x = normed[...]
    last = (((1,), (1,)), ((), ()))
    gate = lax.dot_general(x, wg[...], last, preferred_element_type=jnp.float32)
    upper = lax.dot_general(x, wu[...], last, preferred_element_type=jnp.float32)
    hidden = (jax.nn.silu(gate) * upper).astype(jnp.bfloat16)

    def hop(i, step, t, src):
        way, farthest, nearest = plan[i]
        final = isinstance(step, int) and step == farthest - nearest
        at = pl.ds(t * cols, cols)
        return pltpu.make_async_remote_copy(
            src_ref=src,
            dst_ref=fin.at[i, :, at] if final else buf.at[i, step, :, at],
            send_sem=ssem.at[i, step, t],
            recv_sem=rsem.at[i, step, t],
            device_id={"exp": along(way * nearest if final else way)},
            device_id_type=MESH,
        )

    def chunk(i, step):
        way, farthest, _ = plan[i]
        return (z + way * (farthest - step) + 2 * slots) % slots

    def advance(i, step, t):
        at = pl.ds(t * cols, cols)
        src = buf.at[i, step - 1, :, at]
        hop(i, step - 1, t, src).wait_recv()
        own = part[chunk(i, step), :, at]
        buf[i, step - 1, :, at] = (buf[i, step - 1, :, at].astype(jnp.float32) + own.astype(jnp.float32)).astype(
            jnp.bfloat16
        )
        hop(i, step, t, src).start()

    section = jnp.where(e >= slots, 1, 0)
    tile = width // 4
    for u in range(4):
        span = slice(u * tile, (u + 1) * tile)
        out = jnp.dot(hidden, wd[:, span], preferred_element_type=jnp.float32)
        for b in range(here):
            keep = label_ref[first + b] == section
            kept = jnp.where(keep, out[b * BLOCK:(b + 1) * BLOCK], 0.0)
            part[b * (BLOCK // slot):(b + 1) * (BLOCK // slot), :, span] = kept.reshape(
                BLOCK // slot, slot, tile
            ).astype(jnp.bfloat16)
        for t in range(STREAMS):
            if (u + 1) * STREAMS == 4 * (t + 1):
                for i in range(len(plan)):
                    hop(i, 0, t, part.at[chunk(i, 0), :, pl.ds(t * cols, cols)]).start()

    lengths = [farthest - nearest + 1 for _, farthest, nearest in plan]
    same = min(lengths) - 1

    def step_all(step, carry):
        for t in range(STREAMS):
            for i in range(len(plan)):
                advance(i, step, t)
        return carry

    if same > 1:
        lax.fori_loop(1, same, step_all, 0)
    for step in range(max(same, 1), max(lengths)):
        for t in range(STREAMS):
            for i in range(len(plan)):
                if step < lengths[i]:
                    advance(i, step, t)
    mine = part[z].astype(jnp.float32)
    for i in (2, 3, 0, 1):
        for t in range(STREAMS):
            at = pl.ds(t * cols, cols)
            hop(i, lengths[i] - 1, t, fin.at[i, :, at]).wait_recv()
        mine = mine + fin[i].astype(jnp.float32)
    tw_out[...] = mine.astype(jnp.bfloat16)
    swap = pltpu.make_async_remote_copy(
        src_ref=tw_out, dst_ref=tw_in, send_sem=tsem.at[0], recv_sem=tsem.at[1],
        device_id={"exp": twin}, device_id_type=MESH,
    )
    swap.start()
    swap.wait_recv()
    total = mid[pl.ds(pl.multiple_of(z * slot, slot), slot), :] + (mine + tw_in[...].astype(jnp.float32))
    size = slot // 2
    out_ref[...] = jnp.where(e % 2 == 0, total[:size], total[size:]).astype(jnp.bfloat16)
    swap.wait_send()
    for stage in range(3):
        for kind in range(2):
            for g in range(KV_HEADS):
                piece(stage, kind, g).wait_send()
    for i in range(len(plan)):
        for step in range(lengths[i]):
            for t in range(STREAMS):
                hop(i, step, t, part.at[0, :, pl.ds(t * cols, cols)]).wait_send()


def layer(labels, mask, q, k, v, res, gains, wg, wu, wd, exp_count):
    rows, width = q.shape
    hidden = wg.shape[0]
    slots = exp_count // 2
    slot = rows // slots
    steps = slots // 4
    count = 4 * rows
    half = jnp.bfloat16
    return pl.pallas_call(
        functools.partial(layer_kernel, slots),
        out_shape=jax.ShapeDtypeStruct((slot // 2, width), half),
        in_specs=[SMEM, SMEM, VMEM, ANY, ANY, ANY, ANY, ANY, ANY, ANY],
        out_specs=VMEM,
        scratch_shapes=[
            pltpu.VMEM((rows, width), half),
            pltpu.VMEM((2, KV_HEADS, count, HEAD_DIM), half),
            pltpu.VMEM((rows, width), half),
            pltpu.VMEM((rows, count), jnp.float32),
            pltpu.VMEM((width // HEAD_DIM, rows, 1), jnp.float32),
            pltpu.VMEM((width // HEAD_DIM, rows, 1), jnp.float32),
            pltpu.VMEM((rows, width), jnp.float32),
            pltpu.VMEM((rows, width), half),
            pltpu.VMEM((hidden, width), half),
            pltpu.VMEM((hidden, width), half),
            pltpu.VMEM((hidden, width), half),
            pltpu.VMEM((slots, slot, width), half),
            pltpu.VMEM((4, steps, slot, width), half),
            pltpu.VMEM((4, slot, width), half),
            pltpu.VMEM((slot, width), half),
            pltpu.VMEM((slot, width), half),
            pltpu.SemaphoreType.DMA((5,)),
            pltpu.SemaphoreType.DMA((2, KV_HEADS)),
            pltpu.SemaphoreType.DMA((3, 2, KV_HEADS)),
            pltpu.SemaphoreType.DMA((3, 2, KV_HEADS)),
            pltpu.SemaphoreType.DMA((4, steps, STREAMS)),
            pltpu.SemaphoreType.DMA((4, steps, STREAMS)),
            pltpu.SemaphoreType.DMA((2,)),
            pltpu.SemaphoreType.REGULAR((KV_HEADS,)),
        ],
        compiler_params=pltpu.CompilerParams(
            vmem_limit_bytes=58 * 1024 * 1024, collective_id=1, has_side_effects=True
        ),
        name="layer",
    )(labels, mask, gains, q, k, v, res, wg, wu, wd)


def per_device(queries, keys, values, residual, labels, block_mask, gains, w_gate, w_up, w_down):
    out = layer(
        labels[0], block_mask[0], queries[0], keys[0], values[0], residual[0], gains,
        w_gate.T, w_up.T, w_down, lax.axis_size("exp"),
    )
    return out[None]


def solution(mesh):
    placed = (
        P("dp", "ctx", None),
        P("dp", "ctx", None),
        P("dp", "ctx", None),
        P("dp", "ctx", None),
        P("dp", None),
        P("dp", None, None),
        P(),
        P(None, "exp"),
        P(None, "exp"),
        P("exp", None),
    )
    return jax.shard_map(
        per_device,
        mesh=mesh,
        in_specs=placed,
        out_specs=P("dp", ("ctx", "exp"), None),
        check_vma=False,
    )
```

```python
import functools
import math

import jax
import jax.numpy as jnp
from jax import lax
from jax.experimental import pallas as pl
from jax.experimental.pallas import tpu as pltpu
from jax.sharding import PartitionSpec as P

KV_HEADS = 4
HEAD_DIM = 128
BLOCK = 128
NEG = -1e30
MESH = pl.DeviceIdType.MESH
STREAMS = 4
ANY = pl.BlockSpec(memory_space=pl.ANY)
VMEM = pl.BlockSpec(memory_space=pltpu.VMEM)
SMEM = pl.BlockSpec(memory_space=pltpu.SMEM)


def chains(slots):
    half = slots // 2
    near = half // 2 + half // 16
    return ((1, half - 1, near + 1), (-1, half, near + 1), (1, near, 1), (-1, near, 1))


def layer_kernel(
    slots, label_ref, mask_ref, gain_ref, q_any, k_any, v_any, res_any, wg_any, wu_any, wd_any,
    out_ref, q_ref, kv_ref, res_ref, bias, tops, sums, mid, normed, wg, wu, wd, part,
    buf, fin, tw_in, tw_out, lsem, ksem, kssem, krsem, ssem, rsem, tsem, known,
):
    rows, width = q_ref.shape
    count = kv_ref.shape[2]
    heads = width // HEAD_DIM
    group = heads // KV_HEADS
    here = rows // BLOCK
    slot = rows // slots
    cols = width // STREAMS
    c = lax.axis_index("ctx")
    first = c * here
    e = lax.axis_index("exp")
    z = e // 2
    twin = e + 1 - 2 * (e % 2)
    sib = c + 1 - 2 * (c % 2)
    oth = (c + 2) % 4
    plan = chains(slots)
    reach = plan[0][2]

    def along(distance):
        return (e + 2 * (distance + slots)) % (2 * slots)

    barrier = pltpu.get_barrier_semaphore()
    partners = [{"exp": along(1)}, {"exp": along(-1)}, {"exp": twin}, {"ctx": sib}, {"ctx": oth}]
    partners.append({"ctx": oth, "exp": twin})
    for dev in partners:
        pl.semaphore_signal(barrier, inc=1, device_id=dev, device_id_type=MESH)
    own_loads = [
        pltpu.make_async_copy(
            src.at[:, pl.ds(g * HEAD_DIM, HEAD_DIM)], kv_ref.at[kind, g, pl.ds(0, rows)], ksem.at[kind, g]
        )
        for g in range(KV_HEADS)
        for kind, src in enumerate((k_any, v_any))
    ]
    loads = [
        pltpu.make_async_copy(src, dst, lsem.at[i])
        for i, (src, dst) in enumerate(
            ((q_any, q_ref), (res_any, res_ref), (wg_any, wg), (wu_any, wu), (wd_any, wd))
        )
    ]
    for load in own_loads + loads:
        load.start()
    causal = lax.broadcasted_iota(jnp.int32, (BLOCK, BLOCK), 1) <= lax.broadcasted_iota(
        jnp.int32, (BLOCK, BLOCK), 0
    )
    for b in range(here):
        q_blk = first + b
        for r, shard in enumerate((c, sib, oth, sib + 2 - 4 * (sib // 2))):
            for j in range(here):
                sees = mask_ref[q_blk, shard * here + j] == 1
                lower = jnp.where(sees, 0.0, NEG)
                if r == 0 and j == b:
                    upper = jnp.where(sees & (label_ref[q_blk] == 1), 0.0, NEG)
                    square = jnp.where(causal, lower, upper)
                else:
                    square = jnp.full((BLOCK, BLOCK), lower, jnp.float32)
                at = r * rows + j * BLOCK
                bias[b * BLOCK:(b + 1) * BLOCK, at:at + BLOCK] = square
    for load in own_loads:
        load.wait()

    def piece(stage, kind, g):
        source, target, dev = (
            (0, 2, {"ctx": oth, "exp": twin} if kind else {"ctx": oth}),
            (0, 1, {"ctx": sib}),
            (2, 3, {"ctx": sib}),
        )[stage]
        return pltpu.make_async_remote_copy(
            src_ref=kv_ref.at[kind, g, pl.ds(source * rows, rows)],
            dst_ref=kv_ref.at[kind, g, pl.ds(target * rows, rows)],
            send_sem=kssem.at[stage, kind, g],
            recv_sem=krsem.at[stage, kind, g],
            device_id=dev,
            device_id_type=MESH,
        )

    pl.semaphore_wait(barrier, len(partners))
    for stage in range(2):
        for g in range(KV_HEADS):
            for kind in range(2):
                piece(stage, kind, g).start()

    def tell(i, distance):
        for way in (distance, -distance):
            pl.semaphore_signal(known.at[i], inc=1, device_id={"exp": along(way)}, device_id_type=MESH)

    def learn(i):
        pl.semaphore_wait(known.at[i], 2)

    hops, distance = [], 1
    while distance < reach:
        hops.append(min(distance, reach - distance))
        distance += hops[-1]
    tell(0, hops[0])
    for load in loads[:2]:
        load.wait()
    factor = math.log2(math.e) / math.sqrt(HEAD_DIM)

    def place(h):
        return pl.ds(pl.multiple_of(h * HEAD_DIM, HEAD_DIM), HEAD_DIM)

    def scores_of(h, g, span):
        return lax.dot_general(
            q_ref[:, place(h)], kv_ref[0, g, span], (((1,), (1,)), ((), ())), preferred_element_type=jnp.float32
        ) + bias[:, span]

    def begin(h, carry):
        g = h // group
        scores = scores_of(h, g, slice(0, rows))
        top = jnp.max(scores, axis=-1, keepdims=True)
        weights = jnp.exp2((scores - top) * factor)
        tops[h] = top
        sums[h] = jnp.sum(weights, axis=-1, keepdims=True)
        mid[:, place(h)] = jnp.dot(
            weights.astype(jnp.bfloat16), kv_ref[1, g, 0:rows], preferred_element_type=jnp.float32
        )
        return carry

    lax.fori_loop(0, heads, begin, 0, unroll=4)

    def finish(g, h, squares):
        rest = slice(rows, count)
        scores = scores_of(h, g, rest)
        old = tops[h]
        top = jnp.maximum(old, jnp.max(scores, axis=-1, keepdims=True))
        weights = jnp.exp2((scores - top) * factor)
        shrink = jnp.exp2((old - top) * factor)
        total = sums[h] * shrink + jnp.sum(weights, axis=-1, keepdims=True)
        mixed = mid[:, place(h)] * shrink + jnp.dot(
            weights.astype(jnp.bfloat16), kv_ref[1, g, rest], preferred_element_type=jnp.float32
        )
        x = res_ref[:, place(h)].astype(jnp.float32) + (mixed / total).astype(jnp.bfloat16).astype(jnp.float32)
        mid[:, place(h)] = x
        return squares + x * x

    def forward(g):
        for kind in range(2):
            piece(0, kind, g).wait_recv()
            piece(2, kind, g).start()

    forward(0)
    squares = jnp.zeros((rows, HEAD_DIM), jnp.float32)
    for g in range(KV_HEADS):
        if g + 1 < KV_HEADS:
            forward(g + 1)
        for stage in (1, 2):
            for kind in range(2):
                piece(stage, kind, g).wait_recv()
        if g < len(hops):
            learn(g)
            if g + 1 < len(hops):
                tell(g + 1, hops[g + 1])
        squares = lax.fori_loop(g * group, (g + 1) * group, functools.partial(finish, g), squares, unroll=group)
    inverse = lax.rsqrt(jnp.sum(squares, axis=-1, keepdims=True) / width + 1e-05)
    for b in range(here):
        at = slice(b * BLOCK, (b + 1) * BLOCK)
        visual = label_ref[first + b] == 1
        gain = jnp.where(visual, gain_ref[1:2, :], gain_ref[0:1, :])
        normed[at, :] = (mid[at, :] * inverse[at] * gain).astype(jnp.bfloat16)
    for load in loads[2:]:
        load.wait()
    x = normed[...]
    last = (((1,), (1,)), ((), ()))
    gate = lax.dot_general(x, wg[...], last, preferred_element_type=jnp.float32)
    upper = lax.dot_general(x, wu[...], last, preferred_element_type=jnp.float32)
    hidden = (jax.nn.silu(gate) * upper).astype(jnp.bfloat16)

    def hop(i, step, t, src):
        way, farthest, nearest = plan[i]
        final = isinstance(step, int) and step == farthest - nearest
        at = pl.ds(t * cols, cols)
        return pltpu.make_async_remote_copy(
            src_ref=src,
            dst_ref=fin.at[i, :, at] if final else buf.at[i, step, :, at],
            send_sem=ssem.at[i, step, t],
            recv_sem=rsem.at[i, step, t],
            device_id={"exp": along(way * nearest if final else way)},
            device_id_type=MESH,
        )

    def chunk(i, step):
        way, farthest, _ = plan[i]
        return (z + way * (farthest - step) + 2 * slots) % slots

    def advance(i, step, t):
        at = pl.ds(t * cols, cols)
        src = buf.at[i, step - 1, :, at]
        hop(i, step - 1, t, src).wait_recv()
        own = part[chunk(i, step), :, at]
        buf[i, step - 1, :, at] = (buf[i, step - 1, :, at].astype(jnp.float32) + own.astype(jnp.float32)).astype(
            jnp.bfloat16
        )
        hop(i, step, t, src).start()

    section = jnp.where(e >= slots, 1, 0)
    tile = width // 4
    for u in range(4):
        span = slice(u * tile, (u + 1) * tile)
        out = jnp.dot(hidden, wd[:, span], preferred_element_type=jnp.float32)
        for b in range(here):
            keep = label_ref[first + b] == section
            kept = jnp.where(keep, out[b * BLOCK:(b + 1) * BLOCK], 0.0)
            part[b * (BLOCK // slot):(b + 1) * (BLOCK // slot), :, span] = kept.reshape(
                BLOCK // slot, slot, tile
            ).astype(jnp.bfloat16)
        for t in range(STREAMS):
            if (u + 1) * STREAMS == 4 * (t + 1):
                for i in range(len(plan)):
                    hop(i, 0, t, part.at[chunk(i, 0), :, pl.ds(t * cols, cols)]).start()

    lengths = [farthest - nearest + 1 for _, farthest, nearest in plan]
    same = min(lengths) - 1

    def step_all(step, carry):
        for t in range(STREAMS):
            for i in range(len(plan)):
                advance(i, step, t)
        return carry

    if same > 1:
        lax.fori_loop(1, same, step_all, 0)
    for step in range(max(same, 1), max(lengths)):
        for t in range(STREAMS):
            for i in range(len(plan)):
                if step < lengths[i]:
                    advance(i, step, t)
    mine = part[z].astype(jnp.float32)
    for i in (2, 3, 0, 1):
        for t in range(STREAMS):
            at = pl.ds(t * cols, cols)
            hop(i, lengths[i] - 1, t, fin.at[i, :, at]).wait_recv()
        mine = mine + fin[i].astype(jnp.float32)
    tw_out[...] = mine.astype(jnp.bfloat16)
    swap = pltpu.make_async_remote_copy(
        src_ref=tw_out, dst_ref=tw_in, send_sem=tsem.at[0], recv_sem=tsem.at[1],
        device_id={"exp": twin}, device_id_type=MESH,
    )
    swap.start()
    swap.wait_recv()
    total = mid[pl.ds(pl.multiple_of(z * slot, slot), slot), :] + (mine + tw_in[...].astype(jnp.float32))
    size = slot // 2
    out_ref[...] = jnp.where(e % 2 == 0, total[:size], total[size:]).astype(jnp.bfloat16)
    swap.wait_send()
    for stage in range(3):
        for kind in range(2):
            for g in range(KV_HEADS):
                piece(stage, kind, g).wait_send()
    for i in range(len(plan)):
        for step in range(lengths[i]):
            for t in range(STREAMS):
                hop(i, step, t, part.at[0, :, pl.ds(t * cols, cols)]).wait_send()


def layer(labels, mask, q, k, v, res, gains, wg, wu, wd, exp_count):
    rows, width = q.shape
    hidden = wg.shape[0]
    slots = exp_count // 2
    slot = rows // slots
    steps = max(farthest - nearest + 1 for _, farthest, nearest in chains(slots))
    count = 4 * rows
    half = jnp.bfloat16
    return pl.pallas_call(
        functools.partial(layer_kernel, slots),
        out_shape=jax.ShapeDtypeStruct((slot // 2, width), half),
        in_specs=[SMEM, SMEM, VMEM, ANY, ANY, ANY, ANY, ANY, ANY, ANY],
        out_specs=VMEM,
        scratch_shapes=[
            pltpu.VMEM((rows, width), half),
            pltpu.VMEM((2, KV_HEADS, count, HEAD_DIM), half),
            pltpu.VMEM((rows, width), half),
            pltpu.VMEM((rows, count), jnp.float32),
            pltpu.VMEM((width // HEAD_DIM, rows, 1), jnp.float32),
            pltpu.VMEM((width // HEAD_DIM, rows, 1), jnp.float32),
            pltpu.VMEM((rows, width), jnp.float32),
            pltpu.VMEM((rows, width), half),
            pltpu.VMEM((hidden, width), half),
            pltpu.VMEM((hidden, width), half),
            pltpu.VMEM((hidden, width), half),
            pltpu.VMEM((slots, slot, width), half),
            pltpu.VMEM((4, steps, slot, width), half),
            pltpu.VMEM((4, slot, width), half),
            pltpu.VMEM((slot, width), half),
            pltpu.VMEM((slot, width), half),
            pltpu.SemaphoreType.DMA((5,)),
            pltpu.SemaphoreType.DMA((2, KV_HEADS)),
            pltpu.SemaphoreType.DMA((3, 2, KV_HEADS)),
            pltpu.SemaphoreType.DMA((3, 2, KV_HEADS)),
            pltpu.SemaphoreType.DMA((4, steps, STREAMS)),
            pltpu.SemaphoreType.DMA((4, steps, STREAMS)),
            pltpu.SemaphoreType.DMA((2,)),
            pltpu.SemaphoreType.REGULAR((KV_HEADS,)),
        ],
        compiler_params=pltpu.CompilerParams(
            vmem_limit_bytes=58 * 1024 * 1024, collective_id=1, has_side_effects=True
        ),
        name="layer",
    )(labels, mask, gains, q, k, v, res, wg, wu, wd)


def per_device(queries, keys, values, residual, labels, block_mask, gains, w_gate, w_up, w_down):
    out = layer(
        labels[0], block_mask[0], queries[0], keys[0], values[0], residual[0], gains,
        w_gate.T, w_up.T, w_down, lax.axis_size("exp"),
    )
    return out[None]


def solution(mesh):
    placed = (
        P("dp", "ctx", None),
        P("dp", "ctx", None),
        P("dp", "ctx", None),
        P("dp", "ctx", None),
        P("dp", None),
        P("dp", None, None),
        P(),
        P(None, "exp"),
        P(None, "exp"),
        P("exp", None),
    )
    return jax.shard_map(
        per_device,
        mesh=mesh,
        in_specs=placed,
        out_specs=P("dp", ("ctx", "exp"), None),
        check_vma=False,
    )
```

```python
import functools
import math

import jax
import jax.numpy as jnp
from jax import lax
from jax.experimental import pallas as pl
from jax.experimental.pallas import tpu as pltpu
from jax.sharding import PartitionSpec as P

KV_HEADS = 4
HEAD_DIM = 128
BLOCK = 128
NEG = -1e30
MESH = pl.DeviceIdType.MESH
STREAMS = 2
ANY = pl.BlockSpec(memory_space=pl.ANY)
VMEM = pl.BlockSpec(memory_space=pltpu.VMEM)
SMEM = pl.BlockSpec(memory_space=pltpu.SMEM)


def chains(slots):
    half = slots // 2
    near = half // 2 + half // 16
    return ((1, half - 1, near + 1), (-1, half, near + 1), (1, near, 1), (-1, near, 1))


def layer_kernel(
    slots, label_ref, mask_ref, gain_ref, q_any, k_any, v_any, res_any, wg_any, wu_any, wd_any,
    out_ref, q_ref, kv_ref, res_ref, bias, tops, sums, mid, normed, wg, wu, wd, part,
    pair, buf, fin, tw_in, tw_out, lsem, ksem, kssem, krsem, yssem, yrsem, ssem, rsem, tsem, known,
):
    rows, width = q_ref.shape
    count = kv_ref.shape[2]
    heads = width // HEAD_DIM
    group = heads // KV_HEADS
    here = rows // BLOCK
    slot = rows // slots
    share = width // 2
    cols = share // STREAMS
    c = lax.axis_index("ctx")
    first = c * here
    e = lax.axis_index("exp")
    z = e // 2
    twin = e + 1 - 2 * (e % 2)
    sib = c + 1 - 2 * (c % 2)
    oth = (c + 2) % 4
    plan = chains(slots)
    reach = plan[0][2]

    def along(distance):
        return (e + 2 * (distance + slots)) % (2 * slots)

    barrier = pltpu.get_barrier_semaphore()
    partners = [{"exp": along(1)}, {"exp": along(-1)}, {"exp": twin}, {"ctx": sib}, {"ctx": oth}]
    partners.append({"ctx": oth, "exp": twin})
    for dev in partners:
        pl.semaphore_signal(barrier, inc=1, device_id=dev, device_id_type=MESH)
    own_loads = [
        pltpu.make_async_copy(
            src.at[:, pl.ds(g * HEAD_DIM, HEAD_DIM)], kv_ref.at[kind, g, pl.ds(0, rows)], ksem.at[kind, g]
        )
        for g in range(KV_HEADS)
        for kind, src in enumerate((k_any, v_any))
    ]
    loads = [
        pltpu.make_async_copy(src, dst, lsem.at[i])
        for i, (src, dst) in enumerate(
            ((q_any, q_ref), (res_any, res_ref), (wg_any, wg), (wu_any, wu), (wd_any, wd))
        )
    ]
    for load in own_loads + loads:
        load.start()
    causal = lax.broadcasted_iota(jnp.int32, (BLOCK, BLOCK), 1) <= lax.broadcasted_iota(
        jnp.int32, (BLOCK, BLOCK), 0
    )
    for b in range(here):
        q_blk = first + b
        for r, shard in enumerate((c, sib, oth, sib + 2 - 4 * (sib // 2))):
            for j in range(here):
                sees = mask_ref[q_blk, shard * here + j] == 1
                lower = jnp.where(sees, 0.0, NEG)
                if r == 0 and j == b:
                    upper = jnp.where(sees & (label_ref[q_blk] == 1), 0.0, NEG)
                    square = jnp.where(causal, lower, upper)
                else:
                    square = jnp.full((BLOCK, BLOCK), lower, jnp.float32)
                at = r * rows + j * BLOCK
                bias[b * BLOCK:(b + 1) * BLOCK, at:at + BLOCK] = square
    for load in own_loads:
        load.wait()

    def piece(stage, kind, g):
        source, target, dev = (
            (0, 2, {"ctx": oth, "exp": twin} if kind else {"ctx": oth}),
            (0, 1, {"ctx": sib}),
            (2, 3, {"ctx": sib}),
        )[stage]
        return pltpu.make_async_remote_copy(
            src_ref=kv_ref.at[kind, g, pl.ds(source * rows, rows)],
            dst_ref=kv_ref.at[kind, g, pl.ds(target * rows, rows)],
            send_sem=kssem.at[stage, kind, g],
            recv_sem=krsem.at[stage, kind, g],
            device_id=dev,
            device_id_type=MESH,
        )

    pl.semaphore_wait(barrier, len(partners))
    for stage in range(2):
        for g in range(KV_HEADS):
            for kind in range(2):
                piece(stage, kind, g).start()

    def tell(i, distance):
        for way in (distance, -distance):
            pl.semaphore_signal(known.at[i], inc=1, device_id={"exp": along(way)}, device_id_type=MESH)

    def learn(i):
        pl.semaphore_wait(known.at[i], 2)

    hops, distance = [], 1
    while distance < reach:
        hops.append(min(distance, reach - distance))
        distance += hops[-1]
    tell(0, hops[0])
    for load in loads[:2]:
        load.wait()
    factor = math.log2(math.e) / math.sqrt(HEAD_DIM)

    def place(h):
        return pl.ds(pl.multiple_of(h * HEAD_DIM, HEAD_DIM), HEAD_DIM)

    def scores_of(h, g, span):
        return lax.dot_general(
            q_ref[:, place(h)], kv_ref[0, g, span], (((1,), (1,)), ((), ())), preferred_element_type=jnp.float32
        ) + bias[:, span]

    def begin(h, carry):
        g = h // group
        scores = scores_of(h, g, slice(0, rows))
        top = jnp.max(scores, axis=-1, keepdims=True)
        weights = jnp.exp2((scores - top) * factor)
        tops[h] = top
        sums[h] = jnp.sum(weights, axis=-1, keepdims=True)
        mid[:, place(h)] = jnp.dot(
            weights.astype(jnp.bfloat16), kv_ref[1, g, 0:rows], preferred_element_type=jnp.float32
        )
        return carry

    lax.fori_loop(0, heads, begin, 0, unroll=4)

    def finish(g, h, squares):
        rest = slice(rows, count)
        scores = scores_of(h, g, rest)
        old = tops[h]
        top = jnp.maximum(old, jnp.max(scores, axis=-1, keepdims=True))
        weights = jnp.exp2((scores - top) * factor)
        shrink = jnp.exp2((old - top) * factor)
        total = sums[h] * shrink + jnp.sum(weights, axis=-1, keepdims=True)
        mixed = mid[:, place(h)] * shrink + jnp.dot(
            weights.astype(jnp.bfloat16), kv_ref[1, g, rest], preferred_element_type=jnp.float32
        )
        x = res_ref[:, place(h)].astype(jnp.float32) + (mixed / total).astype(jnp.bfloat16).astype(jnp.float32)
        mid[:, place(h)] = x
        return squares + x * x

    def forward(g):
        for kind in range(2):
            piece(0, kind, g).wait_recv()
            piece(2, kind, g).start()

    forward(0)
    squares = jnp.zeros((rows, HEAD_DIM), jnp.float32)
    for g in range(KV_HEADS):
        if g + 1 < KV_HEADS:
            forward(g + 1)
        for stage in (1, 2):
            for kind in range(2):
                piece(stage, kind, g).wait_recv()
        if g < len(hops):
            learn(g)
            if g + 1 < len(hops):
                tell(g + 1, hops[g + 1])
        squares = lax.fori_loop(g * group, (g + 1) * group, functools.partial(finish, g), squares, unroll=group)
    inverse = lax.rsqrt(jnp.sum(squares, axis=-1, keepdims=True) / width + 1e-05)
    for b in range(here):
        at = slice(b * BLOCK, (b + 1) * BLOCK)
        visual = label_ref[first + b] == 1
        gain = jnp.where(visual, gain_ref[1:2, :], gain_ref[0:1, :])
        normed[at, :] = (mid[at, :] * inverse[at] * gain).astype(jnp.bfloat16)
    for load in loads[2:]:
        load.wait()
    x = normed[...]
    last = (((1,), (1,)), ((), ()))
    gate = lax.dot_general(x, wg[...], last, preferred_element_type=jnp.float32)
    upper = lax.dot_general(x, wu[...], last, preferred_element_type=jnp.float32)
    hidden = (jax.nn.silu(gate) * upper).astype(jnp.bfloat16)

    def hop(i, step, t, src):
        way, farthest, nearest = plan[i]
        final = isinstance(step, int) and step == farthest - nearest
        at = pl.ds(t * cols, cols)
        return pltpu.make_async_remote_copy(
            src_ref=src,
            dst_ref=fin.at[i, :, at] if final else buf.at[i, step, :, at],
            send_sem=ssem.at[i, step, t],
            recv_sem=rsem.at[i, step, t],
            device_id={"exp": along(way * nearest if final else way)},
            device_id_type=MESH,
        )

    def chunk(i, step):
        way, farthest, _ = plan[i]
        return (z + way * (farthest - step) + 2 * slots) % slots

    side = e % 2
    mine_at = pl.multiple_of(side * share, HEAD_DIM)
    lengths = [farthest - nearest + 1 for _, farthest, nearest in plan]
    ahead = 3

    def across(i, step):
        at = z if i == len(plan) else chunk(i, step)
        return pltpu.make_async_remote_copy(
            src_ref=part.at[at, :, pl.ds(pl.multiple_of((1 - side) * share, HEAD_DIM), share)],
            dst_ref=pair.at[at],
            send_sem=yssem.at[i, step],
            recv_sem=yrsem.at[i, step],
            device_id={"exp": twin},
            device_id_type=MESH,
        )

    def across_all(step):
        for i in range(len(plan)):
            if step < lengths[i]:
                across(i, step).start()

    def advance(i, step, t):
        at = pl.ds(t * cols, cols)
        c_at = chunk(i, step)
        if t == 0:
            across(i, step).wait_recv()
        value = part[c_at, :, pl.ds(pl.multiple_of(mine_at + t * cols, HEAD_DIM), cols)].astype(jnp.float32)
        value = value + pair[c_at, :, at].astype(jnp.float32)
        src = pair.at[c_at, :, at]
        if step > 0:
            hop(i, step - 1, t, src).wait_recv()
            value = value + buf[i, step - 1, :, at].astype(jnp.float32)
        pair[c_at, :, at] = value.astype(jnp.bfloat16)
        hop(i, step, t, src).start()

    section = jnp.where(e >= slots, 1, 0)
    tile = width // 4
    for u in range(4):
        span = pl.ds(pl.multiple_of(((2 - 2 * side + u) % 4) * tile, HEAD_DIM), tile)
        out = jnp.dot(hidden, wd[:, span], preferred_element_type=jnp.float32)
        for b in range(here):
            keep = label_ref[first + b] == section
            kept = jnp.where(keep, out[b * BLOCK:(b + 1) * BLOCK], 0.0)
            part[b * (BLOCK // slot):(b + 1) * (BLOCK // slot), :, span] = kept.reshape(
                BLOCK // slot, slot, tile
            ).astype(jnp.bfloat16)
        if u == 1:
            for step in range(ahead):
                across_all(step)
    for step in range(max(lengths)):
        across_all(step + ahead)
        if step + ahead == max(max(lengths) - 1, ahead):
            across(len(plan), 0).start()
        for t in range(STREAMS):
            for i in range(len(plan)):
                if step < lengths[i]:
                    advance(i, step, t)
    across(len(plan), 0).wait_recv()
    mine = part[z, :, pl.ds(mine_at, share)].astype(jnp.float32) + pair[z].astype(jnp.float32)
    for i in (2, 3, 0, 1):
        for t in range(STREAMS):
            at = pl.ds(t * cols, cols)
            hop(i, lengths[i] - 1, t, fin.at[i, :, at]).wait_recv()
        mine = mine + fin[i].astype(jnp.float32)
    tw_out[...] = mine
    swap = pltpu.make_async_remote_copy(
        src_ref=tw_out, dst_ref=tw_in, send_sem=tsem.at[0], recv_sem=tsem.at[1],
        device_id={"exp": twin}, device_id_type=MESH,
    )
    swap.start()
    size = slot // 2

    def put(start, value):
        total = mid[pl.ds(pl.multiple_of(z * slot, slot), slot), pl.ds(start, share)] + value
        out_ref[:, pl.ds(start, share)] = jnp.where(side == 0, total[:size], total[size:]).astype(jnp.bfloat16)

    put(mine_at, mine)
    swap.wait_recv()
    put(pl.multiple_of((1 - side) * share, HEAD_DIM), tw_in[...])
    swap.wait_send()
    across(len(plan), 0).wait_send()
    for i in range(len(plan)):
        for step in range(lengths[i]):
            across(i, step).wait_send()
    for stage in range(3):
        for kind in range(2):
            for g in range(KV_HEADS):
                piece(stage, kind, g).wait_send()
    for i in range(len(plan)):
        for step in range(lengths[i]):
            for t in range(STREAMS):
                hop(i, step, t, pair.at[0, :, pl.ds(t * cols, cols)]).wait_send()


def layer(labels, mask, q, k, v, res, gains, wg, wu, wd, exp_count):
    rows, width = q.shape
    hidden = wg.shape[0]
    slots = exp_count // 2
    slot = rows // slots
    steps = max(farthest - nearest + 1 for _, farthest, nearest in chains(slots))
    count = 4 * rows
    half = jnp.bfloat16
    return pl.pallas_call(
        functools.partial(layer_kernel, slots),
        out_shape=jax.ShapeDtypeStruct((slot // 2, width), half),
        in_specs=[SMEM, SMEM, VMEM, ANY, ANY, ANY, ANY, ANY, ANY, ANY],
        out_specs=VMEM,
        scratch_shapes=[
            pltpu.VMEM((rows, width), half),
            pltpu.VMEM((2, KV_HEADS, count, HEAD_DIM), half),
            pltpu.VMEM((rows, width), half),
            pltpu.VMEM((rows, count), jnp.float32),
            pltpu.VMEM((width // HEAD_DIM, rows, 1), jnp.float32),
            pltpu.VMEM((width // HEAD_DIM, rows, 1), jnp.float32),
            pltpu.VMEM((rows, width), jnp.float32),
            pltpu.VMEM((rows, width), half),
            pltpu.VMEM((hidden, width), half),
            pltpu.VMEM((hidden, width), half),
            pltpu.VMEM((hidden, width), half),
            pltpu.VMEM((slots, slot, width), half),
            pltpu.VMEM((slots, slot, width // 2), half),
            pltpu.VMEM((4, steps, slot, width // 2), half),
            pltpu.VMEM((4, slot, width // 2), half),
            pltpu.VMEM((slot, width // 2), jnp.float32),
            pltpu.VMEM((slot, width // 2), jnp.float32),
            pltpu.SemaphoreType.DMA((5,)),
            pltpu.SemaphoreType.DMA((2, KV_HEADS)),
            pltpu.SemaphoreType.DMA((3, 2, KV_HEADS)),
            pltpu.SemaphoreType.DMA((3, 2, KV_HEADS)),
            pltpu.SemaphoreType.DMA((5, steps)),
            pltpu.SemaphoreType.DMA((5, steps)),
            pltpu.SemaphoreType.DMA((4, steps, STREAMS)),
            pltpu.SemaphoreType.DMA((4, steps, STREAMS)),
            pltpu.SemaphoreType.DMA((2,)),
            pltpu.SemaphoreType.REGULAR((KV_HEADS,)),
        ],
        compiler_params=pltpu.CompilerParams(
            vmem_limit_bytes=58 * 1024 * 1024, collective_id=1, has_side_effects=True
        ),
        name="layer",
    )(labels, mask, gains, q, k, v, res, wg, wu, wd)


def per_device(queries, keys, values, residual, labels, block_mask, gains, w_gate, w_up, w_down):
    out = layer(
        labels[0], block_mask[0], queries[0], keys[0], values[0], residual[0], gains,
        w_gate.T, w_up.T, w_down, lax.axis_size("exp"),
    )
    return out[None]


def solution(mesh):
    placed = (
        P("dp", "ctx", None),
        P("dp", "ctx", None),
        P("dp", "ctx", None),
        P("dp", "ctx", None),
        P("dp", None),
        P("dp", None, None),
        P(),
        P(None, "exp"),
        P(None, "exp"),
        P("exp", None),
    )
    return jax.shard_map(
        per_device,
        mesh=mesh,
        in_specs=placed,
        out_specs=P("dp", ("ctx", "exp"), None),
        check_vma=False,
    )
```

```python
import functools
import math

import jax
import jax.numpy as jnp
from jax import lax
from jax.experimental import pallas as pl
from jax.experimental.pallas import tpu as pltpu
from jax.sharding import PartitionSpec as P

KV_HEADS = 4
HEAD_DIM = 128
BLOCK = 128
NEG = -1e30
MESH = pl.DeviceIdType.MESH
STREAMS = 2
ANY = pl.BlockSpec(memory_space=pl.ANY)
VMEM = pl.BlockSpec(memory_space=pltpu.VMEM)
SMEM = pl.BlockSpec(memory_space=pltpu.SMEM)


def chains(slots):
    half = slots // 2
    near = half // 2 + half // 16
    return ((1, half - 1, near + 1), (-1, half, near + 1), (1, near, 1), (-1, near, 1))


def layer_kernel(
    slots, label_ref, mask_ref, gain_ref, q_any, k_any, v_any, res_any, wg_any, wu_any, wd_any,
    out_ref, q_ref, kv_ref, res_ref, bias, tops, sums, mid, normed, wg, wu, wd, part,
    pair, buf, fin, tw_in, tw_out, lsem, ksem, kssem, krsem, yssem, yrsem, ssem, rsem, tsem, known,
):
    rows, width = q_ref.shape
    count = kv_ref.shape[2]
    heads = width // HEAD_DIM
    group = heads // KV_HEADS
    here = rows // BLOCK
    slot = rows // slots
    share = width // 2
    cols = share // STREAMS
    c = lax.axis_index("ctx")
    first = c * here
    e = lax.axis_index("exp")
    z = e // 2
    twin = e + 1 - 2 * (e % 2)
    sib = c + 1 - 2 * (c % 2)
    oth = (c + 2) % 4
    plan = chains(slots)
    reach = plan[0][2]

    def along(distance):
        return (e + 2 * (distance + slots)) % (2 * slots)

    barrier = pltpu.get_barrier_semaphore()
    partners = [{"exp": along(1)}, {"exp": along(-1)}, {"exp": twin}, {"ctx": sib}, {"ctx": oth}]
    partners.append({"ctx": oth, "exp": twin})
    for dev in partners:
        pl.semaphore_signal(barrier, inc=1, device_id=dev, device_id_type=MESH)
    own_loads = [
        pltpu.make_async_copy(
            src.at[:, pl.ds(g * HEAD_DIM, HEAD_DIM)], kv_ref.at[kind, g, pl.ds(0, rows)], ksem.at[kind, g]
        )
        for g in range(KV_HEADS)
        for kind, src in enumerate((k_any, v_any))
    ]
    loads = [
        pltpu.make_async_copy(src, dst, lsem.at[i])
        for i, (src, dst) in enumerate(
            ((q_any, q_ref), (res_any, res_ref), (wg_any, wg), (wu_any, wu), (wd_any, wd))
        )
    ]
    for load in own_loads + loads:
        load.start()
    causal = lax.broadcasted_iota(jnp.int32, (BLOCK, BLOCK), 1) <= lax.broadcasted_iota(
        jnp.int32, (BLOCK, BLOCK), 0
    )
    for b in range(here):
        q_blk = first + b
        for r, shard in enumerate((c, sib, oth, sib + 2 - 4 * (sib // 2))):
            for j in range(here):
                sees = mask_ref[q_blk, shard * here + j] == 1
                lower = jnp.where(sees, 0.0, NEG)
                if r == 0 and j == b:
                    upper = jnp.where(sees & (label_ref[q_blk] == 1), 0.0, NEG)
                    square = jnp.where(causal, lower, upper)
                else:
                    square = jnp.full((BLOCK, BLOCK), lower, jnp.float32)
                at = r * rows + j * BLOCK
                bias[b * BLOCK:(b + 1) * BLOCK, at:at + BLOCK] = square
    for load in own_loads:
        load.wait()

    def piece(stage, kind, g):
        source, target, dev = (
            (0, 2, {"ctx": oth, "exp": twin} if kind else {"ctx": oth}),
            (0, 1, {"ctx": sib}),
            (2, 3, {"ctx": sib}),
        )[stage]
        return pltpu.make_async_remote_copy(
            src_ref=kv_ref.at[kind, g, pl.ds(source * rows, rows)],
            dst_ref=kv_ref.at[kind, g, pl.ds(target * rows, rows)],
            send_sem=kssem.at[stage, kind, g],
            recv_sem=krsem.at[stage, kind, g],
            device_id=dev,
            device_id_type=MESH,
        )

    pl.semaphore_wait(barrier, len(partners))
    for stage in range(2):
        for g in range(KV_HEADS):
            for kind in range(2):
                piece(stage, kind, g).start()

    def tell(i, distance):
        for way in (distance, -distance):
            pl.semaphore_signal(known.at[i], inc=1, device_id={"exp": along(way)}, device_id_type=MESH)

    def learn(i):
        if i < len(hops):
            pl.semaphore_wait(known.at[i], 2)
        if i + 1 < len(hops):
            tell(i + 1, hops[i + 1])

    hops, distance = [], 1
    while distance < reach:
        hops.append(min(distance, reach - distance))
        distance += hops[-1]
    assert len(hops) <= 4
    tell(0, hops[0])
    for load in loads[:2]:
        load.wait()
    factor = math.log2(math.e) / math.sqrt(HEAD_DIM)

    def place(h):
        return pl.ds(pl.multiple_of(h * HEAD_DIM, HEAD_DIM), HEAD_DIM)

    def scores_of(h, g, span):
        return lax.dot_general(
            q_ref[:, place(h)], kv_ref[0, g, span], (((1,), (1,)), ((), ())), preferred_element_type=jnp.float32
        ) + bias[:, span]

    def begin(h, carry):
        g = h // group
        scores = scores_of(h, g, slice(0, rows))
        top = jnp.max(scores, axis=-1, keepdims=True)
        weights = jnp.exp2((scores - top) * factor)
        tops[h] = top
        sums[h] = jnp.sum(weights, axis=-1, keepdims=True)
        mid[:, place(h)] = jnp.dot(
            weights.astype(jnp.bfloat16), kv_ref[1, g, 0:rows], preferred_element_type=jnp.float32
        )
        return carry

    early = heads // 2
    lax.fori_loop(0, early, begin, 0, unroll=min(early, 7))
    learn(0)
    lax.fori_loop(early, heads, begin, 0, unroll=min(early, 7))

    def finish(g, h, squares):
        rest = slice(rows, count)
        scores = scores_of(h, g, rest)
        old = tops[h]
        top = jnp.maximum(old, jnp.max(scores, axis=-1, keepdims=True))
        weights = jnp.exp2((scores - top) * factor)
        shrink = jnp.exp2((old - top) * factor)
        total = sums[h] * shrink + jnp.sum(weights, axis=-1, keepdims=True)
        mixed = mid[:, place(h)] * shrink + jnp.dot(
            weights.astype(jnp.bfloat16), kv_ref[1, g, rest], preferred_element_type=jnp.float32
        )
        x = res_ref[:, place(h)].astype(jnp.float32) + (mixed / total).astype(jnp.bfloat16).astype(jnp.float32)
        mid[:, place(h)] = x
        return squares + x * x

    def forward(g):
        for kind in range(2):
            piece(0, kind, g).wait_recv()
            piece(2, kind, g).start()

    forward(0)
    squares = jnp.zeros((rows, HEAD_DIM), jnp.float32)
    for g in range(KV_HEADS):
        if g + 1 < KV_HEADS:
            forward(g + 1)
        for stage in (1, 2):
            for kind in range(2):
                piece(stage, kind, g).wait_recv()
        if g in (0, 2):
            learn(1 + g // 2)
        squares = lax.fori_loop(g * group, (g + 1) * group, functools.partial(finish, g), squares, unroll=group)
    inverse = lax.rsqrt(jnp.sum(squares, axis=-1, keepdims=True) / width + 1e-05)
    for b in range(here):
        at = slice(b * BLOCK, (b + 1) * BLOCK)
        visual = label_ref[first + b] == 1
        gain = jnp.where(visual, gain_ref[1:2, :], gain_ref[0:1, :])
        normed[at, :] = (mid[at, :] * inverse[at] * gain).astype(jnp.bfloat16)
    for load in loads[2:]:
        load.wait()
    x = normed[...]
    last = (((1,), (1,)), ((), ()))
    gate = lax.dot_general(x, wg[...], last, preferred_element_type=jnp.float32)
    upper = lax.dot_general(x, wu[...], last, preferred_element_type=jnp.float32)
    hidden = (jax.nn.silu(gate) * upper).astype(jnp.bfloat16)

    def hop(i, step, t, src):
        way, farthest, nearest = plan[i]
        final = isinstance(step, int) and step == farthest - nearest
        at = pl.ds(t * cols, cols)
        return pltpu.make_async_remote_copy(
            src_ref=src,
            dst_ref=fin.at[i, :, at] if final else buf.at[i, step, :, at],
            send_sem=ssem.at[i, step, t],
            recv_sem=rsem.at[i, step, t],
            device_id={"exp": along(way * nearest if final else way)},
            device_id_type=MESH,
        )

    def chunk(i, step):
        way, farthest, _ = plan[i]
        return (z + way * (farthest - step) + 2 * slots) % slots

    side = e % 2
    mine_at = pl.multiple_of(side * share, HEAD_DIM)
    lengths = [farthest - nearest + 1 for _, farthest, nearest in plan]
    ahead = 3

    def across(i, step):
        at = z if i == len(plan) else chunk(i, step)
        return pltpu.make_async_remote_copy(
            src_ref=part.at[at, :, pl.ds(pl.multiple_of((1 - side) * share, HEAD_DIM), share)],
            dst_ref=pair.at[at],
            send_sem=yssem.at[i, step],
            recv_sem=yrsem.at[i, step],
            device_id={"exp": twin},
            device_id_type=MESH,
        )

    def across_all(step):
        for i in range(len(plan)):
            if step < lengths[i]:
                across(i, step).start()

    def advance(i, step, t):
        at = pl.ds(t * cols, cols)
        c_at = chunk(i, step)
        if t == 0:
            across(i, step).wait_recv()
        value = part[c_at, :, pl.ds(pl.multiple_of(mine_at + t * cols, HEAD_DIM), cols)].astype(jnp.float32)
        value = value + pair[c_at, :, at].astype(jnp.float32)
        src = pair.at[c_at, :, at]
        if step > 0:
            hop(i, step - 1, t, src).wait_recv()
            value = value + buf[i, step - 1, :, at].astype(jnp.float32)
        pair[c_at, :, at] = value.astype(jnp.bfloat16)
        hop(i, step, t, src).start()

    learn(3)
    section = jnp.where(e >= slots, 1, 0)
    tile = width // 4
    for u in range(4):
        span = pl.ds(pl.multiple_of(((2 - 2 * side + u) % 4) * tile, HEAD_DIM), tile)
        out = jnp.dot(hidden, wd[:, span], preferred_element_type=jnp.float32)
        for b in range(here):
            keep = label_ref[first + b] == section
            kept = jnp.where(keep, out[b * BLOCK:(b + 1) * BLOCK], 0.0)
            part[b * (BLOCK // slot):(b + 1) * (BLOCK // slot), :, span] = kept.reshape(
                BLOCK // slot, slot, tile
            ).astype(jnp.bfloat16)
        if u == 1:
            for step in range(ahead):
                across_all(step)
    for step in range(max(lengths)):
        across_all(step + ahead)
        if step + ahead == max(max(lengths) - 1, ahead):
            across(len(plan), 0).start()
        for t in range(STREAMS):
            for i in range(len(plan)):
                if step < lengths[i]:
                    advance(i, step, t)
    across(len(plan), 0).wait_recv()
    mine = part[z, :, pl.ds(mine_at, share)].astype(jnp.float32) + pair[z].astype(jnp.float32)
    for i in (2, 3, 0, 1):
        for t in range(STREAMS):
            at = pl.ds(t * cols, cols)
            hop(i, lengths[i] - 1, t, fin.at[i, :, at]).wait_recv()
        mine = mine + fin[i].astype(jnp.float32)
    tw_out[...] = mine
    swap = pltpu.make_async_remote_copy(
        src_ref=tw_out, dst_ref=tw_in, send_sem=tsem.at[0], recv_sem=tsem.at[1],
        device_id={"exp": twin}, device_id_type=MESH,
    )
    swap.start()
    size = slot // 2

    def put(start, value):
        total = mid[pl.ds(pl.multiple_of(z * slot, slot), slot), pl.ds(start, share)] + value
        out_ref[:, pl.ds(start, share)] = jnp.where(side == 0, total[:size], total[size:]).astype(jnp.bfloat16)

    put(mine_at, mine)
    swap.wait_recv()
    put(pl.multiple_of((1 - side) * share, HEAD_DIM), tw_in[...])
    swap.wait_send()
    across(len(plan), 0).wait_send()
    for i in range(len(plan)):
        for step in range(lengths[i]):
            across(i, step).wait_send()
    for stage in range(3):
        for kind in range(2):
            for g in range(KV_HEADS):
                piece(stage, kind, g).wait_send()
    for i in range(len(plan)):
        for step in range(lengths[i]):
            for t in range(STREAMS):
                hop(i, step, t, pair.at[0, :, pl.ds(t * cols, cols)]).wait_send()


def layer(labels, mask, q, k, v, res, gains, wg, wu, wd, exp_count):
    rows, width = q.shape
    hidden = wg.shape[0]
    slots = exp_count // 2
    slot = rows // slots
    steps = max(farthest - nearest + 1 for _, farthest, nearest in chains(slots))
    count = 4 * rows
    half = jnp.bfloat16
    return pl.pallas_call(
        functools.partial(layer_kernel, slots),
        out_shape=jax.ShapeDtypeStruct((slot // 2, width), half),
        in_specs=[SMEM, SMEM, VMEM, ANY, ANY, ANY, ANY, ANY, ANY, ANY],
        out_specs=VMEM,
        scratch_shapes=[
            pltpu.VMEM((rows, width), half),
            pltpu.VMEM((2, KV_HEADS, count, HEAD_DIM), half),
            pltpu.VMEM((rows, width), half),
            pltpu.VMEM((rows, count), jnp.float32),
            pltpu.VMEM((width // HEAD_DIM, rows, 1), jnp.float32),
            pltpu.VMEM((width // HEAD_DIM, rows, 1), jnp.float32),
            pltpu.VMEM((rows, width), jnp.float32),
            pltpu.VMEM((rows, width), half),
            pltpu.VMEM((hidden, width), half),
            pltpu.VMEM((hidden, width), half),
            pltpu.VMEM((hidden, width), half),
            pltpu.VMEM((slots, slot, width), half),
            pltpu.VMEM((slots, slot, width // 2), half),
            pltpu.VMEM((4, steps, slot, width // 2), half),
            pltpu.VMEM((4, slot, width // 2), half),
            pltpu.VMEM((slot, width // 2), jnp.float32),
            pltpu.VMEM((slot, width // 2), jnp.float32),
            pltpu.SemaphoreType.DMA((5,)),
            pltpu.SemaphoreType.DMA((2, KV_HEADS)),
            pltpu.SemaphoreType.DMA((3, 2, KV_HEADS)),
            pltpu.SemaphoreType.DMA((3, 2, KV_HEADS)),
            pltpu.SemaphoreType.DMA((5, steps)),
            pltpu.SemaphoreType.DMA((5, steps)),
            pltpu.SemaphoreType.DMA((4, steps, STREAMS)),
            pltpu.SemaphoreType.DMA((4, steps, STREAMS)),
            pltpu.SemaphoreType.DMA((2,)),
            pltpu.SemaphoreType.REGULAR((KV_HEADS,)),
        ],
        compiler_params=pltpu.CompilerParams(
            vmem_limit_bytes=58 * 1024 * 1024, collective_id=1, has_side_effects=True
        ),
        name="layer",
    )(labels, mask, gains, q, k, v, res, wg, wu, wd)


def per_device(queries, keys, values, residual, labels, block_mask, gains, w_gate, w_up, w_down):
    out = layer(
        labels[0], block_mask[0], queries[0], keys[0], values[0], residual[0], gains,
        w_gate.T, w_up.T, w_down, lax.axis_size("exp"),
    )
    return out[None]


def solution(mesh):
    placed = (
        P("dp", "ctx", None),
        P("dp", "ctx", None),
        P("dp", "ctx", None),
        P("dp", "ctx", None),
        P("dp", None),
        P("dp", None, None),
        P(),
        P(None, "exp"),
        P(None, "exp"),
        P("exp", None),
    )
    return jax.shard_map(
        per_device,
        mesh=mesh,
        in_specs=placed,
        out_specs=P("dp", ("ctx", "exp"), None),
        check_vma=False,
    )
```

```python
import functools
import math

import jax
import jax.numpy as jnp
from jax import lax
from jax.experimental import pallas as pl
from jax.experimental.pallas import tpu as pltpu
from jax.sharding import PartitionSpec as P

KV_HEADS = 4
HEAD_DIM = 128
BLOCK = 128
NEG = -1e30
MESH = pl.DeviceIdType.MESH
STREAMS = 2
ANY = pl.BlockSpec(memory_space=pl.ANY)
VMEM = pl.BlockSpec(memory_space=pltpu.VMEM)
SMEM = pl.BlockSpec(memory_space=pltpu.SMEM)


def chains(slots):
    half = slots // 2
    near = half // 2
    return ((1, half - 1, near + 1), (-1, half, near + 1), (1, near, 1), (-1, near, 1))


def layer_kernel(
    slots, label_ref, mask_ref, gain_ref, q_any, k_any, v_any, res_any, wg_any, wu_any, wd_any,
    out_ref, q_ref, kv_ref, res_ref, bias, tops, sums, mid, normed, wg, wu, wd, part,
    pair, buf, fin, tw_in, tw_out, lsem, ksem, kssem, krsem, yssem, yrsem, ssem, rsem, tsem, known,
):
    rows, width = q_ref.shape
    count = kv_ref.shape[2]
    heads = width // HEAD_DIM
    group = heads // KV_HEADS
    here = rows // BLOCK
    slot = rows // slots
    share = width // 2
    cols = share // STREAMS
    c = lax.axis_index("ctx")
    first = c * here
    e = lax.axis_index("exp")
    z = e // 2
    twin = e + 1 - 2 * (e % 2)
    sib = c + 1 - 2 * (c % 2)
    oth = (c + 2) % 4
    plan = chains(slots)
    reach = plan[0][2]

    def along(distance):
        return (e + 2 * (distance + slots)) % (2 * slots)

    barrier = pltpu.get_barrier_semaphore()
    partners = [{"exp": along(1)}, {"exp": along(-1)}, {"exp": twin}, {"ctx": sib}, {"ctx": oth}]
    partners.append({"ctx": oth, "exp": twin})
    for dev in partners:
        pl.semaphore_signal(barrier, inc=1, device_id=dev, device_id_type=MESH)
    own_loads = [
        pltpu.make_async_copy(
            src.at[:, pl.ds(g * HEAD_DIM, HEAD_DIM)], kv_ref.at[kind, g, pl.ds(0, rows)], ksem.at[kind, g]
        )
        for g in range(KV_HEADS)
        for kind, src in enumerate((k_any, v_any))
    ]
    loads = [
        pltpu.make_async_copy(src, dst, lsem.at[i])
        for i, (src, dst) in enumerate(
            ((q_any, q_ref), (res_any, res_ref), (wg_any, wg), (wu_any, wu), (wd_any, wd))
        )
    ]
    for load in own_loads + loads:
        load.start()
    causal = lax.broadcasted_iota(jnp.int32, (BLOCK, BLOCK), 1) <= lax.broadcasted_iota(
        jnp.int32, (BLOCK, BLOCK), 0
    )
    for b in range(here):
        q_blk = first + b
        for r, shard in enumerate((c, sib, oth, sib + 2 - 4 * (sib // 2))):
            for j in range(here):
                sees = mask_ref[q_blk, shard * here + j] == 1
                lower = jnp.where(sees, 0.0, NEG)
                if r == 0 and j == b:
                    upper = jnp.where(sees & (label_ref[q_blk] == 1), 0.0, NEG)
                    square = jnp.where(causal, lower, upper)
                else:
                    square = jnp.full((BLOCK, BLOCK), lower, jnp.float32)
                at = r * rows + j * BLOCK
                bias[b * BLOCK:(b + 1) * BLOCK, at:at + BLOCK] = square
    for load in own_loads:
        load.wait()

    def piece(stage, kind, g):
        source, target, dev = (
            (0, 2, {"ctx": oth, "exp": twin} if kind else {"ctx": oth}),
            (0, 1, {"ctx": sib}),
            (2, 3, {"ctx": sib}),
        )[stage]
        return pltpu.make_async_remote_copy(
            src_ref=kv_ref.at[kind, g, pl.ds(source * rows, rows)],
            dst_ref=kv_ref.at[kind, g, pl.ds(target * rows, rows)],
            send_sem=kssem.at[stage, kind, g],
            recv_sem=krsem.at[stage, kind, g],
            device_id=dev,
            device_id_type=MESH,
        )

    pl.semaphore_wait(barrier, len(partners))
    for stage in range(2):
        for g in range(KV_HEADS):
            for kind in range(2):
                piece(stage, kind, g).start()

    def tell(i, distance):
        for way in (distance, -distance):
            pl.semaphore_signal(known.at[i], inc=1, device_id={"exp": along(way)}, device_id_type=MESH)

    def learn(i):
        if i < len(hops):
            pl.semaphore_wait(known.at[i], 2)
        if i + 1 < len(hops):
            tell(i + 1, hops[i + 1])

    hops, distance = [], 1
    while distance < reach:
        hops.append(min(distance, reach - distance))
        distance += hops[-1]
    assert len(hops) <= 4
    tell(0, hops[0])
    for load in loads[:2]:
        load.wait()
    factor = math.log2(math.e) / math.sqrt(HEAD_DIM)

    def place(h):
        return pl.ds(pl.multiple_of(h * HEAD_DIM, HEAD_DIM), HEAD_DIM)

    def scores_of(h, g, span):
        return lax.dot_general(
            q_ref[:, place(h)], kv_ref[0, g, span], (((1,), (1,)), ((), ())), preferred_element_type=jnp.float32
        ) + bias[:, span]

    def begin(h, carry):
        g = h // group
        scores = scores_of(h, g, slice(0, rows))
        top = jnp.max(scores, axis=-1, keepdims=True)
        weights = jnp.exp2((scores - top) * factor)
        tops[h] = top
        sums[h] = jnp.sum(weights, axis=-1, keepdims=True)
        mid[:, place(h)] = jnp.dot(
            weights.astype(jnp.bfloat16), kv_ref[1, g, 0:rows], preferred_element_type=jnp.float32
        )
        return carry

    early = heads // 2
    lax.fori_loop(0, early, begin, 0, unroll=min(early, 7))
    learn(0)
    lax.fori_loop(early, heads, begin, 0, unroll=min(early, 7))

    def finish(g, h, squares):
        rest = slice(rows, count)
        scores = scores_of(h, g, rest)
        old = tops[h]
        top = jnp.maximum(old, jnp.max(scores, axis=-1, keepdims=True))
        weights = jnp.exp2((scores - top) * factor)
        shrink = jnp.exp2((old - top) * factor)
        total = sums[h] * shrink + jnp.sum(weights, axis=-1, keepdims=True)
        mixed = mid[:, place(h)] * shrink + jnp.dot(
            weights.astype(jnp.bfloat16), kv_ref[1, g, rest], preferred_element_type=jnp.float32
        )
        x = res_ref[:, place(h)].astype(jnp.float32) + (mixed / total).astype(jnp.bfloat16).astype(jnp.float32)
        mid[:, place(h)] = x
        return squares + x * x

    def forward(g):
        for kind in range(2):
            piece(0, kind, g).wait_recv()
            piece(2, kind, g).start()

    forward(0)
    squares = jnp.zeros((rows, HEAD_DIM), jnp.float32)
    for g in range(KV_HEADS):
        if g + 1 < KV_HEADS:
            forward(g + 1)
        for stage in (1, 2):
            for kind in range(2):
                piece(stage, kind, g).wait_recv()
        if g in (0, 2):
            learn(1 + g // 2)
        squares = lax.fori_loop(g * group, (g + 1) * group, functools.partial(finish, g), squares, unroll=group)
    inverse = lax.rsqrt(jnp.sum(squares, axis=-1, keepdims=True) / width + 1e-05)
    for b in range(here):
        at = slice(b * BLOCK, (b + 1) * BLOCK)
        visual = label_ref[first + b] == 1
        gain = jnp.where(visual, gain_ref[1:2, :], gain_ref[0:1, :])
        normed[at, :] = (mid[at, :] * inverse[at] * gain).astype(jnp.bfloat16)
    for load in loads[2:]:
        load.wait()
    x = normed[...]
    last = (((1,), (1,)), ((), ()))
    gate = lax.dot_general(x, wg[...], last, preferred_element_type=jnp.float32)
    upper = lax.dot_general(x, wu[...], last, preferred_element_type=jnp.float32)
    hidden = (jax.nn.silu(gate) * upper).astype(jnp.bfloat16)

    def hop(i, step, t, src):
        way, farthest, nearest = plan[i]
        final = isinstance(step, int) and step == farthest - nearest
        at = pl.ds(t * cols, cols)
        return pltpu.make_async_remote_copy(
            src_ref=src,
            dst_ref=fin.at[i, :, at] if final else buf.at[i, step, :, at],
            send_sem=ssem.at[i, step, t],
            recv_sem=rsem.at[i, step, t],
            device_id={"exp": along(way * nearest if final else way)},
            device_id_type=MESH,
        )

    def chunk(i, step):
        way, farthest, _ = plan[i]
        return (z + way * (farthest - step) + 2 * slots) % slots

    side = e % 2
    mine_at = pl.multiple_of(side * share, HEAD_DIM)
    lengths = [farthest - nearest + 1 for _, farthest, nearest in plan]
    ahead = 3

    def across(i, step):
        at = z if i == len(plan) else chunk(i, step)
        return pltpu.make_async_remote_copy(
            src_ref=part.at[at, :, pl.ds(pl.multiple_of((1 - side) * share, HEAD_DIM), share)],
            dst_ref=pair.at[at],
            send_sem=yssem.at[i, step],
            recv_sem=yrsem.at[i, step],
            device_id={"exp": twin},
            device_id_type=MESH,
        )

    def across_all(step):
        for i in range(len(plan)):
            if step < lengths[i]:
                across(i, step).start()

    def advance(i, step, t):
        at = pl.ds(t * cols, cols)
        c_at = chunk(i, step)
        if t == 0:
            across(i, step).wait_recv()
        value = part[c_at, :, pl.ds(pl.multiple_of(mine_at + t * cols, HEAD_DIM), cols)].astype(jnp.float32)
        value = value + pair[c_at, :, at].astype(jnp.float32)
        src = pair.at[c_at, :, at]
        if step > 0:
            hop(i, step - 1, t, src).wait_recv()
            value = value + buf[i, step - 1, :, at].astype(jnp.float32)
        pair[c_at, :, at] = value.astype(jnp.bfloat16)
        hop(i, step, t, src).start()

    learn(3)
    section = jnp.where(e >= slots, 1, 0)
    tile = width // 4
    for u in range(4):
        span = pl.ds(pl.multiple_of(((2 - 2 * side + u) % 4) * tile, HEAD_DIM), tile)
        out = jnp.dot(hidden, wd[:, span], preferred_element_type=jnp.float32)
        for b in range(here):
            keep = label_ref[first + b] == section
            kept = jnp.where(keep, out[b * BLOCK:(b + 1) * BLOCK], 0.0)
            part[b * (BLOCK // slot):(b + 1) * (BLOCK // slot), :, span] = kept.reshape(
                BLOCK // slot, slot, tile
            ).astype(jnp.bfloat16)
        if u == 1:
            for step in range(ahead):
                across_all(step)
    for step in range(max(lengths)):
        across_all(step + ahead)
        if step + ahead == max(max(lengths) - 1, ahead):
            across(len(plan), 0).start()
        for t in range(STREAMS):
            for i in range(len(plan)):
                if step < lengths[i]:
                    advance(i, step, t)
    across(len(plan), 0).wait_recv()
    mine = part[z, :, pl.ds(mine_at, share)].astype(jnp.float32) + pair[z].astype(jnp.float32)
    for i in (2, 3, 0, 1):
        for t in range(STREAMS):
            at = pl.ds(t * cols, cols)
            hop(i, lengths[i] - 1, t, fin.at[i, :, at]).wait_recv()
        mine = mine + fin[i].astype(jnp.float32)
    tw_out[...] = mine.astype(jnp.bfloat16)
    swap = pltpu.make_async_remote_copy(
        src_ref=tw_out, dst_ref=tw_in, send_sem=tsem.at[0], recv_sem=tsem.at[1],
        device_id={"exp": twin}, device_id_type=MESH,
    )
    swap.start()
    size = slot // 2

    def put(start, value):
        total = mid[pl.ds(pl.multiple_of(z * slot, slot), slot), pl.ds(start, share)] + value
        out_ref[:, pl.ds(start, share)] = jnp.where(side == 0, total[:size], total[size:]).astype(jnp.bfloat16)

    put(mine_at, mine)
    swap.wait_recv()
    put(pl.multiple_of((1 - side) * share, HEAD_DIM), tw_in[...].astype(jnp.float32))
    swap.wait_send()
    across(len(plan), 0).wait_send()
    for i in range(len(plan)):
        for step in range(lengths[i]):
            across(i, step).wait_send()
    for stage in range(3):
        for kind in range(2):
            for g in range(KV_HEADS):
                piece(stage, kind, g).wait_send()
    for i in range(len(plan)):
        for step in range(lengths[i]):
            for t in range(STREAMS):
                hop(i, step, t, pair.at[0, :, pl.ds(t * cols, cols)]).wait_send()


def layer(labels, mask, q, k, v, res, gains, wg, wu, wd, exp_count):
    rows, width = q.shape
    hidden = wg.shape[0]
    slots = exp_count // 2
    slot = rows // slots
    steps = max(farthest - nearest + 1 for _, farthest, nearest in chains(slots))
    count = 4 * rows
    half = jnp.bfloat16
    return pl.pallas_call(
        functools.partial(layer_kernel, slots),
        out_shape=jax.ShapeDtypeStruct((slot // 2, width), half),
        in_specs=[SMEM, SMEM, VMEM, ANY, ANY, ANY, ANY, ANY, ANY, ANY],
        out_specs=VMEM,
        scratch_shapes=[
            pltpu.VMEM((rows, width), half),
            pltpu.VMEM((2, KV_HEADS, count, HEAD_DIM), half),
            pltpu.VMEM((rows, width), half),
            pltpu.VMEM((rows, count), jnp.float32),
            pltpu.VMEM((width // HEAD_DIM, rows, 1), jnp.float32),
            pltpu.VMEM((width // HEAD_DIM, rows, 1), jnp.float32),
            pltpu.VMEM((rows, width), jnp.float32),
            pltpu.VMEM((rows, width), half),
            pltpu.VMEM((hidden, width), half),
            pltpu.VMEM((hidden, width), half),
            pltpu.VMEM((hidden, width), half),
            pltpu.VMEM((slots, slot, width), half),
            pltpu.VMEM((slots, slot, width // 2), half),
            pltpu.VMEM((4, steps, slot, width // 2), half),
            pltpu.VMEM((4, slot, width // 2), half),
            pltpu.VMEM((slot, width // 2), half),
            pltpu.VMEM((slot, width // 2), half),
            pltpu.SemaphoreType.DMA((5,)),
            pltpu.SemaphoreType.DMA((2, KV_HEADS)),
            pltpu.SemaphoreType.DMA((3, 2, KV_HEADS)),
            pltpu.SemaphoreType.DMA((3, 2, KV_HEADS)),
            pltpu.SemaphoreType.DMA((5, steps)),
            pltpu.SemaphoreType.DMA((5, steps)),
            pltpu.SemaphoreType.DMA((4, steps, STREAMS)),
            pltpu.SemaphoreType.DMA((4, steps, STREAMS)),
            pltpu.SemaphoreType.DMA((2,)),
            pltpu.SemaphoreType.REGULAR((KV_HEADS,)),
        ],
        compiler_params=pltpu.CompilerParams(
            vmem_limit_bytes=58 * 1024 * 1024, collective_id=1, has_side_effects=True
        ),
        name="layer",
    )(labels, mask, gains, q, k, v, res, wg, wu, wd)


def per_device(queries, keys, values, residual, labels, block_mask, gains, w_gate, w_up, w_down):
    out = layer(
        labels[0], block_mask[0], queries[0], keys[0], values[0], residual[0], gains,
        w_gate.T, w_up.T, w_down, lax.axis_size("exp"),
    )
    return out[None]


def solution(mesh):
    placed = (
        P("dp", "ctx", None),
        P("dp", "ctx", None),
        P("dp", "ctx", None),
        P("dp", "ctx", None),
        P("dp", None),
        P("dp", None, None),
        P(),
        P(None, "exp"),
        P(None, "exp"),
        P("exp", None),
    )
    return jax.shard_map(
        per_device,
        mesh=mesh,
        in_specs=placed,
        out_specs=P("dp", ("ctx", "exp"), None),
        check_vma=False,
    )
```
